256 devices in a mesh: pool: 32 (over z_hi, x, y), serve: 8 (over z_lo, core).
Axes of the slice: x: 4, y: 4, z: 8 (z_hi: 2, z_lo: 4; z = z_hi * 4 + z_lo), core: 2. Of those that a mesh axis runs over, the one named last changes fastest.
Arguments:
- queries: bfloat16 [8, 256, 73728], P('serve', None, 'pool'), may hold values from -16 to 16
- new_latent: bfloat16 [8, 147456], P('serve', 'pool'), may hold values from -8 to 8
- pool: bfloat16 [8, 384, 36864], P('serve', 'pool'), may hold values from -6 to 6
- page_owner: int32 [8, 32], P('serve'), may hold values from 0 to 31, as said below
- page_slot: int32 [8, 32], P('serve'), may hold values from 0 to 10
- new_owner: int32 [8, 4], P('serve'), may hold values from 0 to 31, as said below
- new_slot: int32 [8, 4], P('serve'), may hold values from 0 to 11
- prefix_len: int32 [8], P('serve'), may hold values from 512 to 2048, as said below
- w_uv: bfloat16 [128, 512, 128], P('pool', 'serve'), may hold values from -1 to 1
Outputs:
- attn_out: bfloat16 [8, 256, 16384], P('serve', None, 'pool')
- new_pool: bfloat16 [8, 384, 36864], P('serve', 'pool')
The draws below stay inside these ranges and needn't reach their ends.
Inputs may be any that keep to these rules, and one draw needn't show every extreme that they name: Within a request the pairs (page_owner, page_slot) differ from one another and from the pairs (new_owner, new_slot); at most 3 entries of a request's table name the same owner, and in every request some owner is named exactly 3 times. `new_owner`: the 4 new pages of a request go to different owners. `prefix_len`: some request has exactly 2048 prefix tokens.
All inputs are finite; a program needn't handle non-finite values.
Results may differ from the reference program's by a relative error of at most 0.0075.
Values may be sent and summed in bfloat16 or wider, within the bound.
No kernel may reach another device: no remote copies, remote signals or barrier semaphores. Data moves between devices by JAX's collectives and lax.ppermute only.
A program may use at most 128 MiB of HBM per device.

```python
import jax
import jax.numpy as jnp
from jax import lax

HEADS = 128
VLAT = 512
VHEAD = 128
PAGE = 64
SUF = 256
PMAX = 2048
HOT = 3
LAT = 576
PPAGES = 32
NEWP = 4
SLOTS = 12
REQS = 8
N_POOL = 32


def drawn_pair(key):
    folded = jax.random.fold_in(key, 17)
    latent_key, query_key = jax.random.split(folded, 2)
    latent = jax.random.truncated_normal(latent_key, -6.0, 6.0, (REQS, SUF, LAT), jnp.float32)
    queries = jax.random.truncated_normal(query_key, -6.0, 6.0, (REQS, SUF, HEADS, LAT), jnp.float32)
    return (queries.reshape(REQS, SUF, HEADS * LAT), latent.reshape(REQS, SUF * LAT))


def page_tables(key):
    folded = jax.random.fold_in(key, 29)

    def per_request(request_key):
        hot_key, score_key, shuffle_key, slot_key, fresh_key = jax.random.split(request_key, 5)
        owner_key, order_key = jax.random.split(fresh_key)
        tickets = jnp.arange(N_POOL * HOT, dtype=jnp.int32)
        ticket_owner = tickets // HOT
        ticket_rank = tickets % HOT
        hottest = jax.random.randint(hot_key, (), 0, N_POOL, dtype=jnp.int32)
        ticket_score = jax.random.randint(score_key, (N_POOL * HOT,), 0, 1 << 16, dtype=jnp.int32) * (N_POOL * HOT) + tickets
        ticket_score = jnp.where(ticket_owner == hottest, tickets - N_POOL * HOT, ticket_score)
        ordering = jnp.argsort(ticket_score, stable=True)[:PPAGES].astype(jnp.int32)
        ordering = ordering[jax.random.permutation(shuffle_key, PPAGES)]
        page_owners = ticket_owner[ordering]
        page_ranks = ticket_rank[ordering]
        slot_scores = jax.random.randint(slot_key, (N_POOL, SLOTS - 1), 0, 1 << 16, dtype=jnp.int32) * SLOTS + jnp.arange(SLOTS - 1, dtype=jnp.int32)[None, :]
        small_order = jnp.argsort(slot_scores, axis=1, stable=True).astype(jnp.int32)
        last_column = jnp.full((N_POOL, 1), SLOTS - 1, jnp.int32)
        slot_order = jnp.concatenate([small_order[:, :HOT], last_column, small_order[:, HOT:]], 1).astype(jnp.int32)
        page_slots = slot_order[page_owners, page_ranks]
        others = jax.random.permutation(owner_key, N_POOL - 1)[:NEWP - 1].astype(jnp.int32)
        fresh_owners = jnp.concatenate([others, jnp.full((1,), N_POOL - 1, jnp.int32)], 0)
        fresh_owners = fresh_owners[jax.random.permutation(order_key, NEWP)].astype(jnp.int32)
        fresh_slots = slot_order[fresh_owners, HOT + jnp.arange(NEWP, dtype=jnp.int32)]
        return (page_owners, page_slots, fresh_owners, fresh_slots)
    return jax.vmap(per_request)(jax.random.split(folded, REQS))


def draw_queries(key, part):
    return drawn_pair(key)[0].astype(jnp.bfloat16)


def draw_new_latent(key, part):
    return drawn_pair(key)[1].astype(jnp.bfloat16)


def draw_page_owner(key, part):
    return page_tables(key)[0].astype(jnp.int32)


def draw_page_slot(key, part):
    return page_tables(key)[1].astype(jnp.int32)


def draw_new_owner(key, part):
    return page_tables(key)[2].astype(jnp.int32)


def draw_new_slot(key, part):
    return page_tables(key)[3].astype(jnp.int32)


def draw_prefix_len(key, part):
    length_key, top_key = jax.random.split(jax.random.fold_in(key, 41))
    lengths = jax.random.randint(length_key, (REQS,), PMAX // 4, PMAX + 1, dtype=jnp.int32)
    longest = jax.random.randint(top_key, (), 0, REQS, dtype=jnp.int32)
    return jnp.where(jnp.arange(REQS, dtype=jnp.int32) == longest, PMAX, lengths).astype(jnp.int32)


def level_of(own_key, dims, cuts, low, top_value):
    level, own = 1.0, jax.random.fold_in(own_key, 6)
    for dim, blocks in cuts:
        draws = jnp.exp(jax.random.uniform(jax.random.fold_in(own, dim), (blocks,), jnp.float32, low / len(cuts), top_value / len(cuts)))
        level = level * jnp.repeat(draws, dims[dim] // blocks).reshape([-1 if axis == dim else 1 for axis in range(len(dims))])
    return level


def bell_draw(stream_key, extent, spread, limit, pieces=(), kind=jnp.bfloat16):
    loudness = level_of(stream_key, extent, pieces, -0.22, 0.18) if pieces else 1.0
    result = jax.random.normal(stream_key, extent, jnp.float32) * spread * loudness
    return jnp.minimum(jnp.maximum(result, -limit), limit).astype(kind)


def setup_inputs(seed: int = 0) -> dict:
    seeds = jax.random.split(jax.random.key(seed), 10)
    return {
        "queries": draw_queries(jax.random.fold_in(seeds[9], 71), 0),
        "new_latent": draw_new_latent(jax.random.fold_in(seeds[9], 71), 0),
        "pool": bell_draw(seeds[2], (REQS, N_POOL * SLOTS, PAGE * LAT), 1.0, 6.0, ((0, 8), (1, 32))),
        "page_owner": draw_page_owner(jax.random.fold_in(seeds[9], 71), 0),
        "page_slot": draw_page_slot(jax.random.fold_in(seeds[9], 71), 0),
        "new_owner": draw_new_owner(jax.random.fold_in(seeds[9], 71), 0),
        "new_slot": draw_new_slot(jax.random.fold_in(seeds[9], 71), 0),
        "prefix_len": draw_prefix_len(jax.random.fold_in(seeds[9], 71), 0),
        "w_uv": bell_draw(seeds[8], (HEADS, VLAT, VHEAD), (VLAT // 16) ** -0.5, 1.0, ((0, 32), (1, 8))),
    }


softmax_scale = 192.0 ** -0.5
masked_score = -1e30


def reference(queries, new_latent, pool, page_owner, page_slot, new_owner, new_slot, prefix_len, w_uv):
    def per_request(operands):
        query_rows, latent_rows, pool_pages, owners, slot_ids, fresh_owners, fresh_slots, length = operands
        page_rows = (owners * SLOTS + slot_ids).astype(jnp.int32)
        prefix = pool_pages[page_rows].reshape(PPAGES * PAGE, LAT)
        suffix = latent_rows.reshape(SUF, LAT)
        key_rows = jnp.concatenate([prefix, suffix], 0)
        value_rows = key_rows[:, :VLAT]
        position = jnp.arange(PPAGES * PAGE, dtype=jnp.int32)
        earlier = jnp.broadcast_to(position[None, :] < length, (SUF, PPAGES * PAGE))
        query_pos = jnp.arange(SUF, dtype=jnp.int32)
        causal = query_pos[None, :] <= query_pos[:, None]
        allowed = jnp.concatenate([earlier, causal], 1)
        head_queries = query_rows.reshape(SUF, HEADS, LAT).transpose(1, 0, 2)

        def per_head(head_operands):
            one_head, head_weight = head_operands
            scores = jnp.dot(one_head, key_rows.T, preferred_element_type=jnp.float32) * softmax_scale
            scores = jnp.where(allowed, scores, masked_score)
            top_score = jnp.max(scores, axis=1, keepdims=True)
            weights = jnp.exp(scores - top_score)
            weight_sum = jnp.sum(weights, axis=1, keepdims=True)
            mixture = jnp.dot(weights.astype(jnp.bfloat16), value_rows, preferred_element_type=jnp.float32) / weight_sum
            return jnp.dot(mixture.astype(jnp.bfloat16), head_weight, preferred_element_type=jnp.float32).astype(jnp.bfloat16)

        outputs = lax.map(per_head, (head_queries, w_uv))
        attended = outputs.transpose(1, 0, 2).reshape(SUF, HEADS * VHEAD)
        targets = (fresh_owners * SLOTS + fresh_slots).astype(jnp.int32)
        updated = pool_pages.at[targets].set(latent_rows.reshape(NEWP, PAGE * LAT))
        return attended, updated

    attn_out, new_pool = lax.map(per_request, (queries, new_latent, pool, page_owner, page_slot, new_owner, new_slot, prefix_len))
    return attn_out, new_pool
```

```python
import jax
import jax.numpy as jnp
from jax import lax
from jax.experimental import pallas as pl
from jax.experimental.pallas import tpu as pltpu
from jax.sharding import Mesh
from jax.sharding import PartitionSpec as P

VLAT = 512
VHEAD = 128
PAGE = 64
SUF = 256
HOT = 3
LAT = 576
PPAGES = 32
NEWP = 4
SLOTS = 12
PAIR = 2 * LAT
CHUNKS = PAGE * LAT // PAIR
POOL = ("pool_0", "pool_1", "pool_2")
PLANE = ("pool_1", "pool_2")
SIDE = 4
HOPS = (0, 1, 3, 2)
HEAD_ROWS = 40
TAIL_ROWS = 32
KEYS = 16 * (HEAD_ROWS + TAIL_ROWS)

softmax_scale = 192.0 ** (-0.5)
exponent_scale = softmax_scale * 1.4426950408889634
masked_score = -1e30
MIB = 1 << 20


def select_kernel(owner, slot, place, pool_ref, out_ref):
    me = place[0]
    count = jnp.int32(0)
    chosen = [jnp.int32(0)] * HOT
    for j in range(PPAGES):
        hit = owner[j] == me
        chosen = [jnp.where(hit & (count == k), slot[j], chosen[k]) for k in range(HOT)]
        count = count + hit.astype(jnp.int32)
    row = lax.broadcasted_iota(jnp.int32, (8, SLOTS), 0) % 4
    col = lax.broadcasted_iota(jnp.int32, (8, SLOTS), 1)
    want = jnp.where(row == 0, chosen[0], jnp.where(row == 1, chosen[1], chosen[2]))
    pick = ((col == want) & (row < HOT)).astype(jnp.float32).astype(jnp.bfloat16)
    picked = jnp.dot(pick, pool_ref[...], preferred_element_type=jnp.float32)
    upper = lax.broadcasted_iota(jnp.int32, (8, PAIR), 0) < 4
    for d in range(4):
        first = picked[:, 2 * d * PAIR : (2 * d + 1) * PAIR]
        second = picked[:, (2 * d + 1) * PAIR : (2 * d + 2) * PAIR]
        out_ref[d] = jnp.where(upper, first, second).astype(jnp.bfloat16)


def selected_pieces(owner, slot, place, pool):
    return pl.pallas_call(
        select_kernel,
        out_shape=jax.ShapeDtypeStruct((16, 8, PAIR), jnp.bfloat16),
        grid_spec=pltpu.PrefetchScalarGridSpec(
            num_scalar_prefetch=3,
            grid=(4,),
            in_specs=[pl.BlockSpec((SLOTS, 8 * PAIR), lambda i, *_: (0, i))],
            out_specs=pl.BlockSpec((4, 8, PAIR), lambda i, *_: (i, 0, 0)),
        ),
        compiler_params=pltpu.CompilerParams(vmem_limit_bytes=32 * MIB),
        name="select_pages",
    )(owner, slot, place, pool)


def merge_kernel(owner, place, received_ref, suffix_ref, out_ref, count):
    depth = place[0] // 16
    for j in range(PPAGES):
        count[j] = 0
    row = lax.broadcasted_iota(jnp.int32, (PPAGES, 128), 0)
    col = lax.broadcasted_iota(jnp.int32, (PPAGES, 128), 1)
    source = jnp.full((PPAGES, 128), -1, jnp.int32)
    for j in range(PPAGES):
        holder = owner[j]
        rank = count[holder]
        count[holder] = rank + 1
        at = jnp.where(holder // 16 == depth, (holder % 16) * 8 + rank, -8)
        source = jnp.where(row == j, at, source)
    suffix = suffix_ref[...].astype(jnp.float32)
    place_row = lax.broadcasted_iota(jnp.int32, (8, PAIR), 0)
    own = jnp.zeros((8, PAIR), jnp.float32)
    for t in range(4):
        own = jnp.where(place_row == depth * 4 + t, suffix[:, t * PAIR : (t + 1) * PAIR], own)
    received = received_ref[...]
    halves = []
    for p in range(2):
        pick = (col == source + 4 * p).astype(jnp.float32).astype(jnp.bfloat16)
        halves.append(jnp.dot(pick, received, preferred_element_type=jnp.float32))
    rows = jnp.concatenate([halves[0], own, halves[1]], axis=0)
    turned = pltpu.roll(rows[:, VLAT:], LAT, 1)
    out_ref[:, :VLAT] = rows[:, :VLAT].astype(jnp.bfloat16)
    out_ref[:, VLAT : VLAT + 128] = turned[:, VLAT:].astype(jnp.bfloat16)
    out_ref[:, VLAT + 128 :] = turned[:, :VLAT].astype(jnp.bfloat16)


def merged_rows(owner, place, received, suffix):
    rows = HEAD_ROWS + TAIL_ROWS
    return pl.pallas_call(
        merge_kernel,
        out_shape=jax.ShapeDtypeStruct((rows, PAIR), jnp.bfloat16),
        grid_spec=pltpu.PrefetchScalarGridSpec(
            num_scalar_prefetch=2,
            grid=(1,),
            in_specs=[
                pl.BlockSpec((128, PAIR), lambda i, *_: (0, 0)),
                pl.BlockSpec((1, 4 * PAIR), lambda i, *_: (0, 0)),
            ],
            out_specs=pl.BlockSpec((rows, PAIR), lambda i, *_: (0, 0)),
            scratch_shapes=[pltpu.SMEM((PPAGES,), jnp.int32)],
        ),
        compiler_params=pltpu.CompilerParams(vmem_limit_bytes=32 * MIB),
        name="merge_pages",
    )(owner, place, received, suffix)


def shifted(x, axis, hop):
    return lax.ppermute(x, axis, [(i, (i + hop) % SIDE) for i in range(SIDE)])


def gray(s):
    return s ^ (s >> 1)


def limits(parity, x, y, length):
    lane = lax.broadcasted_iota(jnp.int32, (1, KEYS), 1)
    block, part, page = (lane >> 7) & 3, (lane >> 5) & 3, lane & 31
    head = lane < 512
    far = (x - gray(jnp.where(head, part, block))) & 3
    near = (y - gray(jnp.where(head, block, part))) & 3
    token = page * PAGE + (far * 4 + near) * 4 + jnp.where(head, 0, 2) + parity
    seen = jnp.where(token < length, 0, 1 << 20)
    suffix = lane - 1024
    block, part = (suffix >> 5) & 3, (suffix >> 3) & 3
    far, near = (x - gray(part)) & 3, (y - gray(block)) & 3
    holder = ((suffix >> 2) & 1) * 16 + far * 4 + near
    fresh = holder * 8 + (suffix & 3) * 2 + parity
    return jnp.where(lane < 1024, seen, fresh)


def attend_kernel(place, length, q_ref, *refs):
    heads, tails = refs[:4], refs[4:8]
    w_ref, out_ref, keys, even_q, odd_q, limit = refs[8:]

    @pl.when(pl.program_id(0) == 0)
    def _():
        for b in range(4):
            for s in range(4):
                k = 4 * b + s
                keys[k * 32 : (k + 1) * 32] = heads[b][s * HEAD_ROWS : s * HEAD_ROWS + 32]
                keys[1024 + k * 8 : 1024 + (k + 1) * 8] = heads[b][
                    s * HEAD_ROWS + 32 : (s + 1) * HEAD_ROWS
                ]
            keys[512 + b * 128 : 512 + (b + 1) * 128] = tails[b][...]
        lane = lax.broadcasted_iota(jnp.int32, (SUF, 128), 1)
        for h in range(4):
            if h % 2 == 0:
                whole = q_ref[:, h * LAT : h * LAT + LAT + 64].astype(jnp.float32)
            else:
                whole = q_ref[:, h * LAT - 64 : h * LAT + LAT].astype(jnp.float32)
                whole = pltpu.roll(whole, LAT, 1)
            latent = whole[:, :VLAT].astype(jnp.bfloat16)
            tail = whole[:, VLAT:]
            even_q[h, :, :VLAT] = latent
            odd_q[h, :, 128:] = latent
            odd_q[h, :, :128] = jnp.where(lane < 64, tail, 0.0).astype(jnp.bfloat16)
            even_q[h, :, VLAT:] = jnp.where(lane < 64, 0.0, pltpu.roll(tail, 64, 1)).astype(jnp.bfloat16)
        x, y = (place[0] // 4) % 4, place[0] % 4
        for parity in range(2):
            limit[parity : parity + 1] = limits(parity, x, y, length[0])

    h = pl.program_id(0)
    token = lax.broadcasted_iota(jnp.int32, (SUF, 1), 0)
    contract = (((1,), (1,)), ((), ()))
    scores = []
    for parity, queries, cut in ((0, even_q, 0), (1, odd_q, VLAT)):
        s = lax.dot_general(
            queries[h], keys[:, cut : cut + VLAT + 128], contract, preferred_element_type=jnp.float32
        )
        scores.append(jnp.where(limit[parity : parity + 1] <= token, s, masked_score))
    top = jnp.maximum(
        jnp.max(scores[0], axis=1, keepdims=True), jnp.max(scores[1], axis=1, keepdims=True)
    )
    total = jnp.zeros((SUF, 1), jnp.float32)
    mixture = jnp.zeros((SUF, VLAT), jnp.float32)
    for parity, cut in ((0, 0), (1, VLAT + 128)):
        weights = jnp.exp2((scores[parity] - top) * exponent_scale)
        total = total + jnp.sum(weights, axis=1, keepdims=True)
        mixture = mixture + jnp.dot(
            weights.astype(jnp.bfloat16),
            keys[:, cut : cut + VLAT],
            preferred_element_type=jnp.float32,
        )
    mixture = (mixture / total).astype(jnp.bfloat16)
    w = w_ref[...].reshape(VLAT, VHEAD).astype(jnp.bfloat16)
    out_ref[...] = jnp.dot(mixture, w, preferred_element_type=jnp.float32).astype(jnp.bfloat16)


def attended_rows(place, length, queries, heads, tails, w):
    whole = lambda rows: pl.BlockSpec((rows, PAIR), lambda h, *_: (0, 0))
    return pl.pallas_call(
        attend_kernel,
        out_shape=jax.ShapeDtypeStruct((SUF, 4 * VHEAD), jnp.bfloat16),
        grid_spec=pltpu.PrefetchScalarGridSpec(
            num_scalar_prefetch=2,
            grid=(4,),
            in_specs=[
                pl.BlockSpec((SUF, 4 * LAT), lambda h, *_: (0, 0)),
                *[whole(4 * HEAD_ROWS)] * 4,
                *[whole(4 * TAIL_ROWS)] * 4,
                pl.BlockSpec((8, 1, VLAT // 8, VHEAD), lambda h, *_: (0, h, 0, 0)),
            ],
            out_specs=pl.BlockSpec((SUF, VHEAD), lambda h, *_: (0, h)),
            scratch_shapes=[
                pltpu.VMEM((KEYS, PAIR), jnp.bfloat16),
                pltpu.VMEM((4, SUF, VLAT + 128), jnp.bfloat16),
                pltpu.VMEM((4, SUF, VLAT + 128), jnp.bfloat16),
                pltpu.VMEM((2, KEYS), jnp.int32),
            ],
        ),
        compiler_params=pltpu.CompilerParams(vmem_limit_bytes=48 * MIB),
        name="attend",
    )(place, length, queries, *heads, *tails, w)


def update_kernel(place, new_owner, new_slot, pool_ref, *refs):
    heads, out_ref, fresh = refs[:4], refs[4], refs[5]
    me = place[0]
    page, target = jnp.int32(0), jnp.int32(-1)
    for m in range(NEWP):
        hit = new_owner[m] == me
        page = jnp.where(hit, m, page)
        target = jnp.where(hit, new_slot[m], target)
    for b in range(4):
        for s in range(4):
            k = 4 * b + s
            fresh[k * 8 : (k + 1) * 8] = heads[b][s * HEAD_ROWS + 32 : (s + 1) * HEAD_ROWS]
    x, y = (me // 4) % 4, me % 4
    row = lax.broadcasted_iota(jnp.int32, (CHUNKS, 128), 0)
    col = lax.broadcasted_iota(jnp.int32, (CHUNKS, 128), 1)
    holder = page * 8 + (row >> 2)
    part, block = gray((x - (holder >> 2)) & 3), gray((y - holder) & 3)
    source = block * 32 + part * 8 + (holder >> 4) * 4 + (row & 3)
    pick = (col == source).astype(jnp.float32).astype(jnp.bfloat16)
    rows = jnp.dot(pick, fresh[...], preferred_element_type=jnp.float32)
    turned = pltpu.roll(rows[:, VLAT:], LAT, 1)
    rows = jnp.concatenate([rows[:, :VLAT], turned], axis=1)
    mine = lax.broadcasted_iota(jnp.int32, (SLOTS, PAIR), 0) == target
    for c in range(CHUNKS):
        old = pool_ref[:, c * PAIR : (c + 1) * PAIR].astype(jnp.float32)
        out_ref[:, c * PAIR : (c + 1) * PAIR] = jnp.where(mine, rows[c : c + 1], old).astype(jnp.bfloat16)


def updated_pool(place, new_owner, new_slot, pool, heads):
    return pl.pallas_call(
        update_kernel,
        out_shape=jax.ShapeDtypeStruct(pool.shape, pool.dtype),
        grid_spec=pltpu.PrefetchScalarGridSpec(
            num_scalar_prefetch=3,
            grid=(1,),
            in_specs=[
                pl.BlockSpec(pool.shape, lambda i, *_: (0, 0)),
                *[pl.BlockSpec((4 * HEAD_ROWS, PAIR), lambda i, *_: (0, 0))] * 4,
            ],
            out_specs=pl.BlockSpec(pool.shape, lambda i, *_: (0, 0)),
            scratch_shapes=[pltpu.VMEM((128, PAIR), jnp.bfloat16)],
        ),
        compiler_params=pltpu.CompilerParams(vmem_limit_bytes=32 * MIB),
        name="update_pool",
    )(place, new_owner, new_slot, pool, *heads)


def local(queries, new_latent, pool, page_owner, page_slot, new_owner, new_slot, prefix_len, w_uv):
    place = lax.axis_index(POOL).astype(jnp.int32)[None]
    w = lax.all_gather(w_uv.astype(jnp.float32), "serve", axis=0)
    pieces = selected_pieces(page_owner[0], page_slot[0], place, pool[0])
    received = lax.all_to_all(pieces, PLANE, 0, 0, tiled=True).reshape(128, PAIR)
    mine = merged_rows(page_owner[0], place, received, new_latent)
    both = mine + lax.ppermute(mine, "pool_0", [(0, 1), (1, 0)])
    head, tail = both[:HEAD_ROWS], both[HEAD_ROWS:]
    head_row = jnp.concatenate([head] + [shifted(head, "pool_1", k) for k in HOPS[1:]])
    tail_row = jnp.concatenate([tail] + [shifted(tail, "pool_2", k) for k in HOPS[1:]])
    heads = [head_row] + [shifted(head_row, "pool_2", k) for k in HOPS[1:]]
    tails = [tail_row] + [shifted(tail_row, "pool_1", k) for k in HOPS[1:]]
    attended = attended_rows(place, prefix_len, queries[0], heads, tails, w)
    updated = updated_pool(place, new_owner[0], new_slot[0], pool[0], heads)
    return (attended[None], updated[None])


def solution(mesh):
    split = Mesh(
        mesh.devices.reshape(2, 4, 4, mesh.shape["serve"]), ("pool_0", "pool_1", "pool_2", "serve")
    )
    placed = (
        P("serve", None, POOL),
        P("serve", POOL),
        P("serve", POOL, None),
        P("serve", None),
        P("serve", None),
        P("serve", None),
        P("serve", None),
        P("serve"),
        P(POOL, "serve", None),
    )
    return jax.shard_map(
        local,
        mesh=split,
        in_specs=placed,
        out_specs=(P("serve", None, POOL), P("serve", POOL, None)),
        check_vma=False,
    )
```

```python
import jax
import jax.numpy as jnp
from jax import lax
from jax.experimental import pallas as pl
from jax.experimental.pallas import tpu as pltpu
from jax.sharding import Mesh
from jax.sharding import PartitionSpec as P

VLAT = 512
VHEAD = 128
PAGE = 64
SUF = 256
HOT = 3
LAT = 576
PPAGES = 32
NEWP = 4
SLOTS = 12
PAIR = 2 * LAT
CHUNKS = PAGE * LAT // PAIR
POOL = ("pool_0", "pool_1", "pool_2")
PLANE = ("pool_1", "pool_2")
SERVE = ("serve_0", "serve_1")
SIDE = 4
HOPS = (0, 1, 3, 2)
HEAD_ROWS = 40
TAIL_ROWS = 32
KEYS = 16 * (HEAD_ROWS + TAIL_ROWS)

softmax_scale = 192.0 ** (-0.5)
exponent_scale = softmax_scale * 1.4426950408889634
masked_score = -1e30
MIB = 1 << 20


def select_kernel(owner, slot, place, pool_hbm, out_ref, rows, arrived):
    copies = []
    for i in range(4):
        columns = slice(i * 8 * PAIR, (i + 1) * 8 * PAIR)
        copies.append(
            pltpu.make_async_copy(pool_hbm.at[:, columns], rows.at[:, columns], arrived.at[i])
        )
        copies[i].start()
    me = place[0]
    count = jnp.int32(0)
    chosen = [jnp.int32(0)] * HOT
    for j in range(PPAGES):
        hit = owner[0, j] == me
        chosen = [jnp.where(hit & (count == k), slot[0, j], chosen[k]) for k in range(HOT)]
        count = count + hit.astype(jnp.int32)
    row = lax.broadcasted_iota(jnp.int32, (8, SLOTS), 0) % 4
    col = lax.broadcasted_iota(jnp.int32, (8, SLOTS), 1)
    want = jnp.where(row == 0, chosen[0], jnp.where(row == 1, chosen[1], chosen[2]))
    pick = ((col == want) & (row < HOT)).astype(jnp.float32).astype(jnp.bfloat16)
    upper = lax.broadcasted_iota(jnp.int32, (8, PAIR), 0) < 4
    for d in range(16):
        if d % 4 == 0:
            copies[d // 4].wait()
        both = rows[:, 2 * d * PAIR : (2 * d + 2) * PAIR]
        picked = jnp.dot(pick, both, preferred_element_type=jnp.float32)
        out_ref[d] = jnp.where(upper, picked[:, :PAIR], picked[:, PAIR:]).astype(jnp.bfloat16)


def selected_pieces(owner, slot, place, pool):
    return pl.pallas_call(
        select_kernel,
        out_shape=jax.ShapeDtypeStruct((16, 8, PAIR), jnp.bfloat16),
        grid_spec=pltpu.PrefetchScalarGridSpec(
            num_scalar_prefetch=3,
            grid=(1,),
            in_specs=[pl.BlockSpec(memory_space=pltpu.HBM)],
            out_specs=pl.BlockSpec((16, 8, PAIR), lambda i, *_: (0, 0, 0)),
            scratch_shapes=[
                pltpu.VMEM((SLOTS, PAGE * LAT), jnp.bfloat16),
                pltpu.SemaphoreType.DMA((4,)),
            ],
        ),
        compiler_params=pltpu.CompilerParams(vmem_limit_bytes=32 * MIB),
        name="select_pages",
    )(owner, slot, place, pool)


def merge_kernel(owner, place, received_ref, suffix_ref, out_ref, count):
    depth = place[0] // 16
    for j in range(PPAGES):
        count[j] = 0
    row = lax.broadcasted_iota(jnp.int32, (PPAGES, 128), 0)
    col = lax.broadcasted_iota(jnp.int32, (PPAGES, 128), 1)
    source = jnp.full((PPAGES, 128), -1, jnp.int32)
    for j in range(PPAGES):
        holder = owner[0, j]
        rank = count[holder]
        count[holder] = rank + 1
        at = jnp.where(holder // 16 == depth, (holder % 16) * 8 + rank, -8)
        source = jnp.where(row == j, at, source)
    suffix = suffix_ref[...].astype(jnp.float32)
    place_row = lax.broadcasted_iota(jnp.int32, (8, PAIR), 0)
    own = jnp.zeros((8, PAIR), jnp.float32)
    for t in range(4):
        own = jnp.where(place_row == depth * 4 + t, suffix[:, t * PAIR : (t + 1) * PAIR], own)
    received = received_ref[...]
    halves = []
    for p in range(2):
        pick = (col == source + 4 * p).astype(jnp.float32).astype(jnp.bfloat16)
        halves.append(jnp.dot(pick, received, preferred_element_type=jnp.float32))
    rows = jnp.concatenate([halves[0], own, halves[1]], axis=0)
    turned = pltpu.roll(rows[:, VLAT:], LAT, 1)
    out_ref[:, :VLAT] = rows[:, :VLAT].astype(jnp.bfloat16)
    out_ref[:, VLAT : VLAT + 128] = turned[:, VLAT:].astype(jnp.bfloat16)
    out_ref[:, VLAT + 128 :] = turned[:, :VLAT].astype(jnp.bfloat16)


def merged_rows(owner, place, received, suffix):
    rows = HEAD_ROWS + TAIL_ROWS
    return pl.pallas_call(
        merge_kernel,
        out_shape=jax.ShapeDtypeStruct((rows, PAIR), jnp.bfloat16),
        grid_spec=pltpu.PrefetchScalarGridSpec(
            num_scalar_prefetch=2,
            grid=(1,),
            in_specs=[
                pl.BlockSpec((128, PAIR), lambda i, *_: (0, 0)),
                pl.BlockSpec((1, 4 * PAIR), lambda i, *_: (0, 0)),
            ],
            out_specs=pl.BlockSpec((rows, PAIR), lambda i, *_: (0, 0)),
            scratch_shapes=[pltpu.SMEM((PPAGES,), jnp.int32)],
        ),
        compiler_params=pltpu.CompilerParams(vmem_limit_bytes=32 * MIB),
        name="merge_pages",
    )(owner, place, received, suffix)


def shifted(x, axis, hop):
    return lax.ppermute(x, axis, [(i, (i + hop) % SIDE) for i in range(SIDE)])


def gray(s):
    return s ^ (s >> 1)


def spread_kernel(q_ref, even_ref, odd_ref):
    lane = lax.broadcasted_iota(jnp.int32, (SUF, 128), 1)
    for h in range(4):
        if h % 2 == 0:
            whole = q_ref[:, h * LAT : h * LAT + LAT + 64].astype(jnp.float32)
        else:
            whole = q_ref[:, h * LAT - 64 : h * LAT + LAT].astype(jnp.float32)
            whole = pltpu.roll(whole, LAT, 1)
        latent = whole[:, :VLAT].astype(jnp.bfloat16)
        rest = whole[:, VLAT:]
        even_ref[h, :, :VLAT] = latent
        odd_ref[h, :, 128:] = latent
        odd_ref[h, :, :128] = jnp.where(lane < 64, rest, 0.0).astype(jnp.bfloat16)
        even_ref[h, :, VLAT:] = jnp.where(lane < 64, 0.0, pltpu.roll(rest, 64, 1)).astype(jnp.bfloat16)


def spread_queries(queries):
    shape = (4, SUF, VLAT + 128)
    return pl.pallas_call(
        spread_kernel,
        out_shape=[jax.ShapeDtypeStruct(shape, jnp.bfloat16)] * 2,
        grid=(1,),
        in_specs=[pl.BlockSpec((SUF, 4 * LAT), lambda i: (0, 0))],
        out_specs=[pl.BlockSpec(shape, lambda i: (0, 0, 0))] * 2,
        compiler_params=pltpu.CompilerParams(vmem_limit_bytes=32 * MIB),
        cost_estimate=pl.CostEstimate(flops=0, transcendentals=0, bytes_accessed=4 * MIB),
        name="spread_queries",
    )(queries)


def prefix_bias(blocks, parity, x, y, length):
    lane = lax.broadcasted_iota(jnp.int32, (1, 256 * len(blocks)), 1)
    part, page = (lane >> 5) & 3, lane & 31
    index = (lane >> 7) & (len(blocks) - 1)
    hop = jnp.full(lane.shape, HOPS[blocks[0]], jnp.int32)
    for n in range(1, len(blocks)):
        hop = jnp.where(index == n, HOPS[blocks[n]], hop)
    head = lane < 128 * len(blocks)
    turn = gray(part)
    far = (x - jnp.where(head, turn, hop)) & 3
    near = (y - jnp.where(head, hop, turn)) & 3
    token = page * PAGE + (far * 4 + near) * 4 + jnp.where(head, 0, 2) + parity
    return jnp.where(token < length, 0.0, masked_score)


def suffix_order(parity, x, y):
    lane = lax.broadcasted_iota(jnp.int32, (1, 128), 1)
    block, part = lane >> 5, (lane >> 3) & 3
    far, near = (x - gray(part)) & 3, (y - gray(block)) & 3
    holder = ((lane >> 2) & 1) * 16 + far * 4 + near
    return holder * 8 + (lane & 3) * 2 + parity


def attend_kernel(blocks, first, last, place, length, even_q, odd_q, *refs):
    n = len(blocks)
    refs = list(refs)
    heads, tails = [refs.pop(0) for _ in range(n)], [refs.pop(0) for _ in range(n)]
    others = [refs.pop(0) for _ in range(4 - n)] if last else []
    weights_in = [refs.pop(0) for _ in range(2)] if last else []
    before = [] if first else [refs.pop(0) for _ in range(2)]
    after = [refs.pop(0) for _ in range(1 if last else 2)]
    keys = refs[0]
    pages = 256 * n

    for b in range(n):
        for t in range(4):
            row = b * 128 + t * 32
            keys[row : row + 32] = heads[b][t * HEAD_ROWS : t * HEAD_ROWS + 32]
        keys[(n + b) * 128 : (n + b + 1) * 128] = tails[b][...]
    x, y = (place[0] // 4) % 4, place[0] % 4
    bias = [prefix_bias(blocks, parity, x, y, length[0]) for parity in range(2)]
    if last:
        w = refs[1]
        for b, head in enumerate([*others, *heads]):
            for t in range(4):
                row = pages + b * 32 + t * 8
                keys[row : row + 8] = head[t * HEAD_ROWS + 32 : (t + 1) * HEAD_ROWS]
        token = lax.broadcasted_iota(jnp.int32, (SUF, 128), 0)
        hidden = [suffix_order(parity, x, y) > token for parity in range(2)]
        for k in range(4):
            for other in range(2):
                part = ((place[1] // 2 - HOPS[k]) & 3) * 2 + ((place[1] & 1) ^ other)
                rows = pl.ds(pl.multiple_of(part * (VLAT // 8), VLAT // 8), VLAT // 8)
                w[:, rows, :] = weights_in[other][k]

    def scored(h):
        pieces = []
        for parity, queries, cut in ((0, even_q, 0), (1, odd_q, VLAT)):
            s = lax.dot_general(
                queries[h],
                keys[:, cut : cut + VLAT + 128],
                (((1,), (1,)), ((), ())),
                preferred_element_type=jnp.float32,
            )
            if last:
                fresh = jnp.where(hidden[parity], masked_score, s[:, pages:])
                s = jnp.concatenate([s[:, :pages] + bias[parity], fresh], axis=1)
            else:
                s = s + bias[parity]
            pieces.append(s)
        return pieces

    def mixed(h, pieces):
        top = jnp.max(jnp.maximum(pieces[0], pieces[1]), axis=1, keepdims=True)
        if not first:
            top_old, total_old = before[1][h, :, :1], before[1][h, :, 1:2]
            top = jnp.maximum(top, top_old)
        weights = [jnp.exp2((piece - top) * exponent_scale) for piece in pieces]
        total = jnp.sum(weights[0] + weights[1], axis=1, keepdims=True)
        parts = [
            jnp.dot(
                weights[parity].astype(jnp.bfloat16),
                keys[:, cut : cut + VLAT],
                preferred_element_type=jnp.float32,
            )
            for parity, cut in ((0, 0), (1, VLAT + 128))
        ]
        mixture = parts[0] + parts[1]
        if not first:
            rescale = jnp.exp2((top_old - top) * exponent_scale)
            total = total + total_old * rescale
            mixture = mixture + before[0][h] * rescale
        if last:
            mixture = (mixture / total).astype(jnp.bfloat16)
            out = jnp.dot(mixture, w[h], preferred_element_type=jnp.float32)
            after[0][:, h * VHEAD : (h + 1) * VHEAD] = out.astype(jnp.bfloat16)
        else:
            after[0][h] = mixture
            lane = lax.broadcasted_iota(jnp.int32, (SUF, 128), 1)
            after[1][h] = jnp.where(lane == 0, top, total)

    pieces = scored(0)
    for h in range(4):
        following = scored(h + 1) if h < 3 else None
        mixed(h, pieces)
        pieces = following


def attended(blocks, place, length, spread, heads, tails, state, w):
    n, first, last = len(blocks), not state, bool(w)
    whole = lambda *shape: pl.BlockSpec(shape, lambda h, *_: (0,) * len(shape))
    state_specs = [whole(4, SUF, VLAT), whole(4, SUF, 128)]
    own_heads, own_tails = [heads[b] for b in blocks], [tails[b] for b in blocks]
    others = [heads[b] for b in range(4) if b not in blocks] if last else []
    rows = 256 * n + (128 if last else 0)
    scratch = [pltpu.VMEM((rows, PAIR), jnp.bfloat16)]
    if last:
        out_shape = jax.ShapeDtypeStruct((SUF, 4 * VHEAD), jnp.bfloat16)
        out_specs = whole(SUF, 4 * VHEAD)
        scratch.append(pltpu.VMEM((4, VLAT, VHEAD), jnp.bfloat16))
    else:
        out_shape = [
            jax.ShapeDtypeStruct((4, SUF, VLAT), jnp.float32),
            jax.ShapeDtypeStruct((4, SUF, 128), jnp.float32),
        ]
        out_specs = state_specs

    def kernel(*refs):
        attend_kernel(blocks, first, last, *refs)

    return pl.pallas_call(
        kernel,
        out_shape=out_shape,
        grid_spec=pltpu.PrefetchScalarGridSpec(
            num_scalar_prefetch=2,
            grid=(1,),
            in_specs=[
                *[whole(4, SUF, VLAT + 128)] * 2,
                *[whole(4 * HEAD_ROWS, PAIR)] * n,
                *[whole(4 * TAIL_ROWS, PAIR)] * n,
                *[whole(4 * HEAD_ROWS, PAIR)] * len(others),
                *([whole(4, 4, VLAT // 8, VHEAD)] * 2 if last else []),
                *([] if first else state_specs),
            ],
            out_specs=out_specs,
            scratch_shapes=scratch,
        ),
        compiler_params=pltpu.CompilerParams(vmem_limit_bytes=40 * MIB),
        cost_estimate=pl.CostEstimate(
            flops=8 * SUF * rows * (2 * VLAT + 128) * 2,
            transcendentals=8 * SUF * rows,
            bytes_accessed=16 * MIB,
        ),
        name="attend_" + "".join(str(b) for b in blocks),
    )(place, length, *spread, *own_heads, *own_tails, *others, *w, *state)


def update_kernel(place, new_owner, new_slot, pool_ref, *refs):
    heads, out_ref, fresh = refs[:4], refs[4], refs[5]
    me = place[0]
    page, target = jnp.int32(0), jnp.int32(-1)
    for m in range(NEWP):
        hit = new_owner[0, m] == me
        page = jnp.where(hit, m, page)
        target = jnp.where(hit, new_slot[0, m], target)
    for b in range(4):
        for s in range(4):
            k = 4 * b + s
            fresh[k * 8 : (k + 1) * 8] = heads[b][s * HEAD_ROWS + 32 : (s + 1) * HEAD_ROWS]
    x, y = (me // 4) % 4, me % 4
    row = lax.broadcasted_iota(jnp.int32, (CHUNKS, 128), 0)
    col = lax.broadcasted_iota(jnp.int32, (CHUNKS, 128), 1)
    holder = page * 8 + (row >> 2)
    part, block = gray((x - (holder >> 2)) & 3), gray((y - holder) & 3)
    source = block * 32 + part * 8 + (holder >> 4) * 4 + (row & 3)
    pick = (col == source).astype(jnp.float32).astype(jnp.bfloat16)
    rows = jnp.dot(pick, fresh[...], preferred_element_type=jnp.float32)
    turned = pltpu.roll(rows[:, VLAT:], LAT, 1)
    rows = jnp.concatenate([rows[:, :VLAT], turned], axis=1)
    mine = lax.broadcasted_iota(jnp.int32, (SLOTS, PAIR), 0) == target
    for c in range(CHUNKS):
        old = pool_ref[:, c * PAIR : (c + 1) * PAIR].astype(jnp.float32)
        out_ref[:, c * PAIR : (c + 1) * PAIR] = jnp.where(mine, rows[c : c + 1], old).astype(jnp.bfloat16)


def updated_pool(place, new_owner, new_slot, pool, heads):
    return pl.pallas_call(
        update_kernel,
        out_shape=jax.ShapeDtypeStruct(pool.shape, pool.dtype),
        grid_spec=pltpu.PrefetchScalarGridSpec(
            num_scalar_prefetch=3,
            grid=(1,),
            in_specs=[
                pl.BlockSpec(pool.shape, lambda i, *_: (0, 0)),
                *[pl.BlockSpec((4 * HEAD_ROWS, PAIR), lambda i, *_: (0, 0))] * 4,
            ],
            out_specs=pl.BlockSpec(pool.shape, lambda i, *_: (0, 0)),
            scratch_shapes=[pltpu.VMEM((128, PAIR), jnp.bfloat16)],
        ),
        compiler_params=pltpu.CompilerParams(vmem_limit_bytes=32 * MIB),
        cost_estimate=pl.CostEstimate(flops=0, transcendentals=0, bytes_accessed=6 * MIB),
        name="update_pool",
    )(place, new_owner, new_slot, pool, *heads)


def local(queries, new_latent, pool, page_owner, page_slot, new_owner, new_slot, prefix_len, w_uv):
    place = jnp.stack([lax.axis_index(POOL), lax.axis_index(SERVE)]).astype(jnp.int32)
    w_row = jnp.stack([w_uv] + [shifted(w_uv, "serve_0", k) for k in HOPS[1:]])
    pieces = selected_pieces(page_owner, page_slot, place, pool[0])
    received = lax.all_to_all(pieces, PLANE, 0, 0, tiled=True).reshape(128, PAIR)
    mine = merged_rows(page_owner, place, received, new_latent)
    mine, queries, w_row = lax.optimization_barrier((mine, queries, w_row))
    w = [w_row, lax.ppermute(w_row, "serve_1", [(0, 1), (1, 0)])]
    spread = spread_queries(queries[0])
    both = mine + lax.ppermute(mine, "pool_0", [(0, 1), (1, 0)])
    head, tail = both[:HEAD_ROWS], both[HEAD_ROWS:]
    head_row = jnp.concatenate([head] + [shifted(head, "pool_1", k) for k in HOPS[1:]])
    tail_row = jnp.concatenate([tail] + [shifted(tail, "pool_2", k) for k in HOPS[1:]])
    head_row, tail_row, *w = lax.optimization_barrier((head_row, tail_row, *w))
    state = attended((0,), place, prefix_len, spread, [head_row], [tail_row], (), ())
    state, late = lax.optimization_barrier((state, tail_row))
    tail_far = shifted(late, "pool_1", HOPS[3])
    head_far = shifted(head_row, "pool_2", HOPS[3])
    tails = [tail_row] + [shifted(tail_row, "pool_1", k) for k in HOPS[1:3]] + [tail_far]
    heads = [head_row] + [shifted(head_row, "pool_2", k) for k in HOPS[1:3]] + [head_far]
    state = attended((1, 2), place, prefix_len, spread, heads, tails, state, ())
    out = attended((3,), place, prefix_len, spread, heads, tails, state, w)
    updated = updated_pool(place, new_owner, new_slot, pool[0], heads)
    return (out[None], updated[None])


def solution(mesh):
    shape = (2, SIDE, SIDE, SIDE, 2)
    split = Mesh(mesh.devices.reshape(shape), (*POOL, *SERVE))
    placed = (
        P(SERVE, None, POOL),
        P(SERVE, POOL),
        P(SERVE, POOL, None),
        P(SERVE, None),
        P(SERVE, None),
        P(SERVE, None),
        P(SERVE, None),
        P(SERVE),
        P(POOL, SERVE, None),
    )
    return jax.shard_map(
        local,
        mesh=split,
        in_specs=placed,
        out_specs=(P(SERVE, None, POOL), P(SERVE, POOL, None)),
        check_vma=False,
    )
```

```python
import jax
import jax.numpy as jnp
from jax import lax
from jax.experimental import pallas as pl
from jax.experimental.pallas import tpu as pltpu
from jax.sharding import Mesh
from jax.sharding import PartitionSpec as P

VLAT = 512
VHEAD = 128
PAGE = 64
SUF = 256
HOT = 3
LAT = 576
PPAGES = 32
NEWP = 4
SLOTS = 12
PAIR = 2 * LAT
CHUNKS = PAGE * LAT // PAIR
POOL = ("pool_0", "pool_1", "pool_2")
PLANE = ("pool_1", "pool_2")
SERVE = ("serve_0", "serve_1")
SIDE = 4
HOPS = (0, 1, 3, 2)
HEAD_ROWS = 40
TAIL_ROWS = 32
KEYS = 16 * (HEAD_ROWS + TAIL_ROWS)

softmax_scale = 192.0 ** (-0.5)
exponent_scale = softmax_scale * 1.4426950408889634
masked_score = -1e30
MIB = 1 << 20


def select_kernel(owner, slot, place, pool_hbm, out_ref, rows, arrived):
    copies = []
    for i in range(4):
        columns = slice(i * 8 * PAIR, (i + 1) * 8 * PAIR)
        copies.append(
            pltpu.make_async_copy(pool_hbm.at[:, columns], rows.at[:, columns], arrived.at[i])
        )
        copies[i].start()
    me = place[0]
    count = jnp.int32(0)
    chosen = [jnp.int32(0)] * HOT
    for j in range(PPAGES):
        hit = owner[0, j] == me
        chosen = [jnp.where(hit & (count == k), slot[0, j], chosen[k]) for k in range(HOT)]
        count = count + hit.astype(jnp.int32)
    row = lax.broadcasted_iota(jnp.int32, (8, SLOTS), 0) % 4
    col = lax.broadcasted_iota(jnp.int32, (8, SLOTS), 1)
    want = jnp.where(row == 0, chosen[0], jnp.where(row == 1, chosen[1], chosen[2]))
    pick = ((col == want) & (row < HOT)).astype(jnp.float32).astype(jnp.bfloat16)
    upper = lax.broadcasted_iota(jnp.int32, (8, PAIR), 0) < 4
    for d in range(16):
        if d % 4 == 0:
            copies[d // 4].wait()
        both = rows[:, 2 * d * PAIR : (2 * d + 2) * PAIR]
        picked = jnp.dot(pick, both, preferred_element_type=jnp.float32)
        out_ref[d] = jnp.where(upper, picked[:, :PAIR], picked[:, PAIR:]).astype(jnp.bfloat16)


def selected_pieces(owner, slot, place, pool):
    return pl.pallas_call(
        select_kernel,
        out_shape=jax.ShapeDtypeStruct((16, 8, PAIR), jnp.bfloat16),
        grid_spec=pltpu.PrefetchScalarGridSpec(
            num_scalar_prefetch=3,
            grid=(1,),
            in_specs=[pl.BlockSpec(memory_space=pltpu.HBM)],
            out_specs=pl.BlockSpec((16, 8, PAIR), lambda i, *_: (0, 0, 0)),
            scratch_shapes=[
                pltpu.VMEM((SLOTS, PAGE * LAT), jnp.bfloat16),
                pltpu.SemaphoreType.DMA((4,)),
            ],
        ),
        compiler_params=pltpu.CompilerParams(vmem_limit_bytes=32 * MIB),
        name="select_pages",
    )(owner, slot, place, pool)


def merge_kernel(owner, place, received_ref, suffix_ref, out_ref, count):
    depth = place[0] // 16
    for j in range(PPAGES):
        count[j] = 0
    row = lax.broadcasted_iota(jnp.int32, (PPAGES, 128), 0)
    col = lax.broadcasted_iota(jnp.int32, (PPAGES, 128), 1)
    source = jnp.full((PPAGES, 128), -1, jnp.int32)
    for j in range(PPAGES):
        holder = owner[0, j]
        rank = count[holder]
        count[holder] = rank + 1
        at = jnp.where(holder // 16 == depth, (holder % 16) * 8 + rank, -8)
        source = jnp.where(row == j, at, source)
    suffix = suffix_ref[...].astype(jnp.float32)
    place_row = lax.broadcasted_iota(jnp.int32, (8, PAIR), 0)
    own = jnp.zeros((8, PAIR), jnp.float32)
    for t in range(4):
        own = jnp.where(place_row == depth * 4 + t, suffix[:, t * PAIR : (t + 1) * PAIR], own)
    received = received_ref[...]
    halves = []
    for p in range(2):
        pick = (col == source + 4 * p).astype(jnp.float32).astype(jnp.bfloat16)
        halves.append(jnp.dot(pick, received, preferred_element_type=jnp.float32))
    rows = jnp.concatenate([halves[0], own, halves[1]], axis=0)
    turned = pltpu.roll(rows[:, VLAT:], LAT, 1)
    out_ref[:, :VLAT] = rows[:, :VLAT].astype(jnp.bfloat16)
    out_ref[:, VLAT : VLAT + 128] = turned[:, VLAT:].astype(jnp.bfloat16)
    out_ref[:, VLAT + 128 :] = turned[:, :VLAT].astype(jnp.bfloat16)


def merged_rows(owner, place, received, suffix):
    rows = HEAD_ROWS + TAIL_ROWS
    return pl.pallas_call(
        merge_kernel,
        out_shape=jax.ShapeDtypeStruct((rows, PAIR), jnp.bfloat16),
        grid_spec=pltpu.PrefetchScalarGridSpec(
            num_scalar_prefetch=2,
            grid=(1,),
            in_specs=[
                pl.BlockSpec((128, PAIR), lambda i, *_: (0, 0)),
                pl.BlockSpec((1, 4 * PAIR), lambda i, *_: (0, 0)),
            ],
            out_specs=pl.BlockSpec((rows, PAIR), lambda i, *_: (0, 0)),
            scratch_shapes=[pltpu.SMEM((PPAGES,), jnp.int32)],
        ),
        compiler_params=pltpu.CompilerParams(vmem_limit_bytes=32 * MIB),
        name="merge_pages",
    )(owner, place, received, suffix)


def shifted(x, axis, hop):
    return lax.ppermute(x, axis, [(i, (i + hop) % SIDE) for i in range(SIDE)])


def gray(s):
    return s ^ (s >> 1)


def spread_kernel(q_ref, even_ref, odd_ref):
    lane = lax.broadcasted_iota(jnp.int32, (SUF, 128), 1)
    for h in range(4):
        if h % 2 == 0:
            whole = q_ref[:, h * LAT : h * LAT + LAT + 64].astype(jnp.float32)
        else:
            whole = q_ref[:, h * LAT - 64 : h * LAT + LAT].astype(jnp.float32)
            whole = pltpu.roll(whole, LAT, 1)
        latent = whole[:, :VLAT].astype(jnp.bfloat16)
        rest = whole[:, VLAT:]
        even_ref[h, :, :VLAT] = latent
        odd_ref[h, :, 128:] = latent
        odd_ref[h, :, :128] = jnp.where(lane < 64, rest, 0.0).astype(jnp.bfloat16)
        even_ref[h, :, VLAT:] = jnp.where(lane < 64, 0.0, pltpu.roll(rest, 64, 1)).astype(jnp.bfloat16)


def spread_queries(queries):
    shape = (4, SUF, VLAT + 128)
    return pl.pallas_call(
        spread_kernel,
        out_shape=[jax.ShapeDtypeStruct(shape, jnp.bfloat16)] * 2,
        grid=(1,),
        in_specs=[pl.BlockSpec((SUF, 4 * LAT), lambda i: (0, 0))],
        out_specs=[pl.BlockSpec(shape, lambda i: (0, 0, 0))] * 2,
        compiler_params=pltpu.CompilerParams(vmem_limit_bytes=32 * MIB),
        cost_estimate=pl.CostEstimate(flops=0, transcendentals=0, bytes_accessed=4 * MIB),
        name="spread_queries",
    )(queries)


def prefix_bias(blocks, parity, x, y, length):
    lane = lax.broadcasted_iota(jnp.int32, (1, 256 * len(blocks)), 1)
    part, page = (lane >> 5) & 3, lane & 31
    index = (lane >> 7) & (len(blocks) - 1)
    hop = jnp.full(lane.shape, HOPS[blocks[0]], jnp.int32)
    for n in range(1, len(blocks)):
        hop = jnp.where(index == n, HOPS[blocks[n]], hop)
    head = lane < 128 * len(blocks)
    turn = gray(part)
    far = (x - jnp.where(head, turn, hop)) & 3
    near = (y - jnp.where(head, hop, turn)) & 3
    token = page * PAGE + (far * 4 + near) * 4 + jnp.where(head, 0, 2) + parity
    return jnp.where(token < length, 0.0, masked_score)


def suffix_order(x, y):
    lane = lax.broadcasted_iota(jnp.int32, (1, SUF), 1)
    block, part = (lane >> 5) & 3, (lane >> 3) & 3
    far, near = (x - gray(part)) & 3, (y - gray(block)) & 3
    holder = ((lane >> 2) & 1) * 16 + far * 4 + near
    return holder * 8 + (lane & 3) * 2 + (lane >> 7)


def new_page(place, new_owner, new_slot):
    page, target = jnp.int32(0), jnp.int32(-1)
    for m in range(NEWP):
        hit = new_owner[0, m] == place[0]
        page = jnp.where(hit, m, page)
        target = jnp.where(hit, new_slot[0, m], target)
    return page, target


def write_page(place, page, target, fresh, slots):
    x, y = (place[0] // 4) % 4, place[0] % 4
    row = lax.broadcasted_iota(jnp.int32, (CHUNKS, 128), 0)
    col = lax.broadcasted_iota(jnp.int32, (CHUNKS, 128), 1)
    holder = page * 8 + (row >> 2)
    part, block = gray((x - (holder >> 2)) & 3), gray((y - holder) & 3)
    source = block * 32 + part * 8 + (holder >> 4) * 4 + (row & 3)
    pick = (col == source).astype(jnp.float32).astype(jnp.bfloat16)
    rows = jnp.dot(pick, fresh, preferred_element_type=jnp.float32)
    rows = jnp.concatenate([rows[:, :VLAT], pltpu.roll(rows[:, VLAT:], LAT, 1)], axis=1)
    for low, high in ((0, 8), (8, SLOTS)):

        @pl.when((target >= low) & (target < high))
        def _():
            mine = lax.broadcasted_iota(jnp.int32, (high - low, PAIR), 0) + low == target
            for c in range(CHUNKS):
                columns = slice(c * PAIR, (c + 1) * PAIR)
                old = slots[low:high, columns].astype(jnp.float32)
                slots[low:high, columns] = jnp.where(mine, rows[c : c + 1], old).astype(jnp.bfloat16)


def segment(parts, t, rows):
    part, at = divmod(t * len(parts), 4)
    start = at // len(parts) * rows
    return parts[part][start : start + rows]


def attend_kernel(blocks, first, last, *refs):
    n = len(blocks)
    refs = list(refs)
    take = lambda count: [refs.pop(0) for _ in range(count)]
    place, length = take(2)
    new_owner, new_slot = take(2) if last else (None, None)
    even_q, odd_q = take(2)
    if last:
        heads, tails, others = [take(2)], [take(2)], [[ref] for ref in take(3)]
        weights_in, pool = take(2), take(1)[0]
    else:
        heads, tails = [[ref] for ref in take(n)], [[ref] for ref in take(n)]
    before = [] if first else take(2)
    after = take(2)
    keys = take(1)[0]

    if last:
        fresh, suffix, w, slots, moved = refs
        fill = pltpu.make_async_copy(pool, slots, moved.at[0])
        flush = pltpu.make_async_copy(slots, after[1], moved.at[1])
        fill.start()
    for b in range(n):
        for t in range(4):
            row = b * 128 + t * 32
            keys[row : row + 32] = segment(heads[b], t, HEAD_ROWS)[:32]
            row = (n + b) * 128 + t * 32
            keys[row : row + 32] = segment(tails[b], t, TAIL_ROWS)
    x, y = (place[0] // 4) % 4, place[0] % 4
    bias = [prefix_bias(blocks, parity, x, y, length[0]) for parity in range(2)]
    if last:
        for b, head in enumerate([*others, *heads]):
            for t in range(4):
                row = b * 32 + t * 8
                fresh[row : row + 8] = segment(head, t, HEAD_ROWS)[32:]
        suffix[:128] = fresh[:, : VLAT + 128]
        suffix[128:, :VLAT] = fresh[:, VLAT + 128 :]
        ropes = fresh[:, VLAT : VLAT + 128].astype(jnp.float32)
        suffix[128:, VLAT:] = pltpu.roll(ropes, 64, 1).astype(jnp.bfloat16)
        token = lax.broadcasted_iota(jnp.int32, (SUF, SUF), 0)
        hidden = suffix_order(x, y) > token
        for k in range(4):
            for other in range(2):
                part = ((place[1] // 2 - HOPS[k]) & 3) * 2 + ((place[1] & 1) ^ other)
                rows = pl.ds(pl.multiple_of(part * (VLAT // 8), VLAT // 8), VLAT // 8)
                w[:, rows, :] = weights_in[other][k]

    even = slice(0, VLAT), slice(0, VLAT + 128)
    odd = slice(VLAT + 128, PAIR), slice(VLAT, PAIR)
    groups = [(even_q, keys, even), (odd_q, keys, odd)]
    if last:
        groups.append((even_q, suffix, even))

    def scored(h):
        pieces = []
        for g, (queries, rows, (_, columns)) in enumerate(groups):
            s = lax.dot_general(
                queries[h], rows[:, columns], (((1,), (1,)), ((), ())), preferred_element_type=jnp.float32
            )
            pieces.append(jnp.where(hidden, masked_score, s) if g == 2 else s + bias[g])
        return pieces

    def mixed(h, pieces):
        top = pieces[0]
        for piece in pieces[1:]:
            top = jnp.maximum(top, piece)
        top = jnp.max(top, axis=1, keepdims=True)
        if not first:
            top_old, total_old = before[1][h, :, :1], before[1][h, :, 1:2]
            top = jnp.maximum(top, top_old)
        weights = [jnp.exp2((piece - top) * exponent_scale) for piece in pieces]
        total = jnp.sum(sum(weights[1:], weights[0]), axis=1, keepdims=True)
        parts = [
            jnp.dot(weight.astype(jnp.bfloat16), rows[:, columns], preferred_element_type=jnp.float32)
            for weight, (_, rows, (columns, _)) in zip(weights, groups)
        ]
        mixture = sum(parts[1:], parts[0])
        if not first:
            rescale = jnp.exp2((top_old - top) * exponent_scale)
            total = total + total_old * rescale
            mixture = mixture + before[0][h] * rescale
        if last:
            mixture = (mixture * (1.0 / total)).astype(jnp.bfloat16)
            out = jnp.dot(mixture, w[h], preferred_element_type=jnp.float32)
            after[0][:, h * VHEAD : (h + 1) * VHEAD] = out.astype(jnp.bfloat16)
        else:
            after[0][h] = mixture
            lane = lax.broadcasted_iota(jnp.int32, (SUF, 128), 1)
            after[1][h] = jnp.where(lane == 0, top, total)

    pieces = scored(0)
    for h in range(4):
        following = scored(h + 1) if h < 3 else None
        mixed(h, pieces)
        pieces = following
        if last and h == 1:
            page, target = new_page(place, new_owner, new_slot)
            fill.wait()

            @pl.when(target >= 0)
            def _():
                write_page(place, page, target, fresh[...], slots)

            flush.start()
    if last:
        flush.wait()


def attended(blocks, place, length, spread, heads, tails, state, ending=()):
    n, first, last = len(blocks), not state, bool(ending)
    whole = lambda *shape: pl.BlockSpec(shape, lambda h, *_: (0,) * len(shape))
    in_hbm = pl.BlockSpec(memory_space=pltpu.HBM)
    state_specs = [whole(4, SUF, VLAT), whole(4, SUF, 128)]
    own_heads, own_tails = ([a for b in blocks for a in parts[b]] for parts in (heads, tails))
    others, w, tables, pool = [], [], (), []
    scratch = [pltpu.VMEM((256 * n, PAIR), jnp.bfloat16)]
    if last:
        w, new_owner, new_slot, pool = ending
        tables, pool = (new_owner, new_slot), [pool]
        others = [a for b in range(4) if b not in blocks for a in heads[b]]
        out_shape = [
            jax.ShapeDtypeStruct((SUF, 4 * VHEAD), jnp.bfloat16),
            jax.ShapeDtypeStruct((SLOTS, PAGE * LAT), jnp.bfloat16),
        ]
        out_specs = [whole(SUF, 4 * VHEAD), in_hbm]
        scratch += [
            pltpu.VMEM((128, PAIR), jnp.bfloat16),
            pltpu.VMEM((SUF, VLAT + 128), jnp.bfloat16),
            pltpu.VMEM((4, VLAT, VHEAD), jnp.bfloat16),
            pltpu.VMEM((SLOTS, PAGE * LAT), jnp.bfloat16),
            pltpu.SemaphoreType.DMA((2,)),
        ]
    else:
        out_shape = [
            jax.ShapeDtypeStruct((4, SUF, VLAT), jnp.float32),
            jax.ShapeDtypeStruct((4, SUF, 128), jnp.float32),
        ]
        out_specs = state_specs

    def kernel(*refs):
        attend_kernel(blocks, first, last, *refs)

    keys = 256 * n + (128 if last else 0)
    return pl.pallas_call(
        kernel,
        out_shape=out_shape,
        grid_spec=pltpu.PrefetchScalarGridSpec(
            num_scalar_prefetch=2 + len(tables),
            grid=(1,),
            in_specs=[
                *[whole(4, SUF, VLAT + 128)] * 2,
                *[whole(*a.shape) for a in (*own_heads, *own_tails, *others)],
                *[whole(4, 4, VLAT // 8, VHEAD)] * len(w),
                *[in_hbm] * len(pool),
                *([] if first else state_specs),
            ],
            out_specs=out_specs,
            scratch_shapes=scratch,
        ),
        compiler_params=pltpu.CompilerParams(vmem_limit_bytes=40 * MIB),
        cost_estimate=pl.CostEstimate(
            flops=8 * SUF * keys * (2 * VLAT + 128) * 2,
            transcendentals=8 * SUF * keys,
            bytes_accessed=16 * MIB,
        ),
        name="attend_" + "".join(str(b) for b in blocks),
    )(place, length, *tables, *spread, *own_heads, *own_tails, *others, *w, *pool, *state)


def local(queries, new_latent, pool, page_owner, page_slot, new_owner, new_slot, prefix_len, w_uv):
    place = jnp.stack([lax.axis_index(POOL), lax.axis_index(SERVE)]).astype(jnp.int32)
    w_row = jnp.stack([w_uv] + [shifted(w_uv, "serve_0", k) for k in HOPS[1:]])
    page_owner, page_slot, new_owner, new_slot, in_place = (
        pltpu.with_memory_space_constraint(a, pltpu.HBM)
        for a in (page_owner, page_slot, new_owner, new_slot, pool[0])
    )
    pieces = selected_pieces(page_owner, page_slot, place, in_place)
    received = lax.all_to_all(pieces, PLANE, 0, 0, tiled=True).reshape(128, PAIR)
    mine = merged_rows(page_owner, place, received, new_latent)
    mine, queries = lax.optimization_barrier((mine, queries))
    spread = spread_queries(queries[0])
    both = mine + lax.ppermute(mine, "pool_0", [(0, 1), (1, 0)])
    both, w_row = lax.optimization_barrier((both, w_row))
    w = [w_row, lax.ppermute(w_row, "serve_1", [(0, 1), (1, 0)])]
    head, tail = both[:HEAD_ROWS], both[HEAD_ROWS:]
    head_parts = [shifted(head, "pool_1", k) for k in HOPS[1:]]
    tail_parts = [shifted(tail, "pool_2", k) for k in HOPS[1:]]
    head_parts, tail_parts[:2] = lax.optimization_barrier((head_parts, tail_parts[:2]))
    head_row = jnp.concatenate([head, *head_parts])
    tail_row = jnp.concatenate([tail, *tail_parts])
    tail_row, *w = lax.optimization_barrier((tail_row, *w))
    heads, tails = [[head_row]], [[tail_row]]
    state = attended((0,), place, prefix_len, spread, heads, tails, ())
    for rows, axis in ((heads, "pool_2"), (tails, "pool_1")):
        rows += [[shifted(rows[0][0], axis, k)] for k in HOPS[1:3]]
        half = rows[0][0].shape[0] // 2
        rows.append([shifted(rows[1][0][:half], axis, 1), shifted(rows[2][0][half:], axis, 3)])
    state = attended((1, 2), place, prefix_len, spread, heads, tails, state)
    ending = (w, new_owner, new_slot, in_place)
    out, updated = attended((3,), place, prefix_len, spread, heads, tails, state, ending)
    return (out[None], updated[None])


def solution(mesh):
    shape = (2, SIDE, SIDE, SIDE, 2)
    split = Mesh(mesh.devices.reshape(shape), (*POOL, *SERVE))
    placed = (
        P(SERVE, None, POOL),
        P(SERVE, POOL),
        P(SERVE, POOL, None),
        P(SERVE, None),
        P(SERVE, None),
        P(SERVE, None),
        P(SERVE, None),
        P(SERVE),
        P(POOL, SERVE, None),
    )
    return jax.shard_map(
        local,
        mesh=split,
        in_specs=placed,
        out_specs=(P(SERVE, None, POOL), P(SERVE, POOL, None)),
        check_vma=False,
    )
```

```python
import jax
import jax.numpy as jnp
from jax import lax
from jax.experimental import pallas as pl
from jax.experimental.pallas import tpu as pltpu
from jax.sharding import Mesh
from jax.sharding import PartitionSpec as P

VLAT = 512
VHEAD = 128
PAGE = 64
SUF = 256
HOT = 3
LAT = 576
PPAGES = 32
NEWP = 4
SLOTS = 12
PAIR = 2 * LAT
CHUNKS = PAGE * LAT // PAIR
POOL = ("pool_0", "pool_1", "pool_2")
PLANE = ("pool_1", "pool_2")
SERVE = ("serve_0", "serve_1")
SIDE = 4
HOPS = (0, 1, 3, 2)
HEAD_ROWS = 40
TAIL_ROWS = 32
KEYS = 16 * (HEAD_ROWS + TAIL_ROWS)

softmax_scale = 192.0 ** (-0.5)
exponent_scale = softmax_scale * 1.4426950408889634
masked_score = -1e30
MIB = 1 << 20


def select_kernel(place, owner_hbm, slot_hbm, pool_hbm, suffix_hbm, *refs):
    out_ref, source_ref, own_ref, rows, fresh, owner, slot, count, arrived = refs
    copies = [
        pltpu.make_async_copy(owner_hbm, owner, arrived.at[4]),
        pltpu.make_async_copy(slot_hbm, slot, arrived.at[5]),
        pltpu.make_async_copy(suffix_hbm, fresh, arrived.at[6]),
    ]
    for i in range(4):
        columns = slice(i * 8 * PAIR, (i + 1) * 8 * PAIR)
        copies.append(
            pltpu.make_async_copy(pool_hbm.at[:, columns], rows.at[:, columns], arrived.at[i])
        )
    for copy in copies:
        copy.start()
    me, depth = place[0], place[0] // 16
    for j in range(PPAGES):
        count[j] = 0
    copies[0].wait()
    copies[1].wait()
    row = lax.broadcasted_iota(jnp.int32, (PPAGES, 128), 0)
    source = jnp.full((PPAGES, 128), -8, jnp.int32)
    chosen = [jnp.int32(0)] * HOT
    for j in range(PPAGES):
        holder = owner[0, j]
        rank = count[holder]
        count[holder] = rank + 1
        chosen = [jnp.where((holder == me) & (rank == k), slot[0, j], chosen[k]) for k in range(HOT)]
        at = jnp.where(holder // 16 == depth, (holder % 16) * 8 + rank, -8)
        source = jnp.where(row == j, at, source)
    source_ref[...] = source
    copies[2].wait()
    suffix = fresh[...].astype(jnp.float32)
    row = lax.broadcasted_iota(jnp.int32, (8, PAIR), 0)
    own = jnp.zeros((8, PAIR), jnp.float32)
    for t in range(4):
        own = jnp.where(row == depth * 4 + t, suffix[:, t * PAIR : (t + 1) * PAIR], own)
    own_ref[...] = own
    row = lax.broadcasted_iota(jnp.int32, (8, SLOTS), 0) % 4
    col = lax.broadcasted_iota(jnp.int32, (8, SLOTS), 1)
    want = jnp.where(row == 0, chosen[0], jnp.where(row == 1, chosen[1], chosen[2]))
    pick = ((col == want) & (row < HOT)).astype(jnp.float32).astype(jnp.bfloat16)
    upper = lax.broadcasted_iota(jnp.int32, (8, PAIR), 0) < 4
    for d in range(16):
        if d % 4 == 0:
            copies[3 + d // 4].wait()
        both = rows[:, 2 * d * PAIR : (2 * d + 2) * PAIR]
        picked = jnp.dot(pick, both, preferred_element_type=jnp.float32)
        out_ref[d] = jnp.where(upper, picked[:, :PAIR], picked[:, PAIR:]).astype(jnp.bfloat16)


def selected_pieces(place, owner, slot, pool, suffix):
    in_hbm = pl.BlockSpec(memory_space=pltpu.HBM)
    whole = lambda *shape: pl.BlockSpec(shape, lambda i, *_: (0,) * len(shape))
    return pl.pallas_call(
        select_kernel,
        out_shape=[
            jax.ShapeDtypeStruct((16, 8, PAIR), jnp.bfloat16),
            jax.ShapeDtypeStruct((PPAGES, 128), jnp.int32),
            jax.ShapeDtypeStruct((8, PAIR), jnp.float32),
        ],
        grid_spec=pltpu.PrefetchScalarGridSpec(
            num_scalar_prefetch=1,
            grid=(1,),
            in_specs=[in_hbm] * 4,
            out_specs=[whole(16, 8, PAIR), whole(PPAGES, 128), whole(8, PAIR)],
            scratch_shapes=[
                pltpu.VMEM((SLOTS, PAGE * LAT), jnp.bfloat16),
                pltpu.VMEM((1, 4 * PAIR), jnp.bfloat16),
                pltpu.SMEM((1, PPAGES), jnp.int32),
                pltpu.SMEM((1, PPAGES), jnp.int32),
                pltpu.SMEM((PPAGES,), jnp.int32),
                pltpu.SemaphoreType.DMA((7,)),
            ],
        ),
        compiler_params=pltpu.CompilerParams(vmem_limit_bytes=32 * MIB),
        name="select_pages",
    )(place, owner, slot, pool, suffix)


def merge_kernel(received_ref, source_ref, own_ref, out_ref):
    col = lax.broadcasted_iota(jnp.int32, (PPAGES, 128), 1)
    received = received_ref[...]
    halves = []
    for p in range(2):
        pick = (col == source_ref[...] + 4 * p).astype(jnp.float32).astype(jnp.bfloat16)
        halves.append(jnp.dot(pick, received, preferred_element_type=jnp.float32))
    rows = jnp.concatenate([halves[0], own_ref[...], halves[1]], axis=0)
    turned = pltpu.roll(rows[:, VLAT:], LAT, 1)
    out_ref[:, :VLAT] = rows[:, :VLAT].astype(jnp.bfloat16)
    out_ref[:, VLAT : VLAT + 128] = turned[:, VLAT:].astype(jnp.bfloat16)
    out_ref[:, VLAT + 128 :] = turned[:, :VLAT].astype(jnp.bfloat16)


def merged_rows(received, source, own):
    whole = lambda *shape: pl.BlockSpec(shape, lambda i: (0,) * len(shape))
    rows = HEAD_ROWS + TAIL_ROWS
    return pl.pallas_call(
        merge_kernel,
        out_shape=jax.ShapeDtypeStruct((rows, PAIR), jnp.bfloat16),
        grid=(1,),
        in_specs=[whole(128, PAIR), whole(PPAGES, 128), whole(8, PAIR)],
        out_specs=whole(rows, PAIR),
        compiler_params=pltpu.CompilerParams(vmem_limit_bytes=32 * MIB),
        name="merge_pages",
    )(received, source, own)


def shifted(x, axis, hop):
    return lax.ppermute(x, axis, [(i, (i + hop) % SIDE) for i in range(SIDE)])


def mirrored(x, axis, hop):
    places = [(i, core) for i in range(SIDE) for core in range(2)]
    pairs = [(2 * i + c, 2 * ((i + hop * (1 - 2 * c)) % SIDE) + c) for i, c in places]
    return lax.ppermute(x, (axis, "serve_1"), pairs)


def gray(s):
    return s ^ (s >> 1)


def spread_kernel(q_ref, even_ref, odd_ref):
    lane = lax.broadcasted_iota(jnp.int32, (SUF, 128), 1)
    for h in range(4):
        if h % 2 == 0:
            whole = q_ref[:, h * LAT : h * LAT + LAT + 64].astype(jnp.float32)
        else:
            whole = q_ref[:, h * LAT - 64 : h * LAT + LAT].astype(jnp.float32)
            whole = pltpu.roll(whole, LAT, 1)
        latent = whole[:, :VLAT].astype(jnp.bfloat16)
        rest = whole[:, VLAT:]
        even_ref[h, :, :VLAT] = latent
        odd_ref[h, :, 128:] = latent
        odd_ref[h, :, :128] = jnp.where(lane < 64, rest, 0.0).astype(jnp.bfloat16)
        even_ref[h, :, VLAT:] = jnp.where(lane < 64, 0.0, pltpu.roll(rest, 64, 1)).astype(jnp.bfloat16)


def spread_queries(queries):
    shape = (4, SUF, VLAT + 128)
    return pl.pallas_call(
        spread_kernel,
        out_shape=[jax.ShapeDtypeStruct(shape, jnp.bfloat16)] * 2,
        grid=(1,),
        in_specs=[pl.BlockSpec((SUF, 4 * LAT), lambda i: (0, 0))],
        out_specs=[pl.BlockSpec(shape, lambda i: (0, 0, 0))] * 2,
        compiler_params=pltpu.CompilerParams(vmem_limit_bytes=32 * MIB),
        cost_estimate=pl.CostEstimate(flops=0, transcendentals=0, bytes_accessed=4 * MIB),
        name="spread_queries",
    )(queries)


def prefix_bias(blocks, parity, x, y, way, length):
    lane = lax.broadcasted_iota(jnp.int32, (1, 256 * len(blocks)), 1)
    part, page = (lane >> 5) & 3, lane & 31
    index = (lane >> 7) & (len(blocks) - 1)
    hop = jnp.full(lane.shape, HOPS[blocks[0]], jnp.int32)
    for n in range(1, len(blocks)):
        hop = jnp.where(index == n, HOPS[blocks[n]], hop)
    head = lane < 128 * len(blocks)
    turn = gray(part)
    hop = hop * way
    far = (x - jnp.where(head, turn, hop)) & 3
    near = (y - jnp.where(head, hop, turn)) & 3
    token = page * PAGE + (far * 4 + near) * 4 + jnp.where(head, 0, 2) + parity
    return jnp.where(token < length, 0.0, masked_score)


def suffix_order(x, y, way):
    lane = lax.broadcasted_iota(jnp.int32, (1, SUF), 1)
    block, part = (lane >> 5) & 3, (lane >> 3) & 3
    far, near = (x - gray(part)) & 3, (y - gray(block) * way) & 3
    holder = ((lane >> 2) & 1) * 16 + far * 4 + near
    return holder * 8 + (lane & 3) * 2 + (lane >> 7)


def new_page(place, new_owner, new_slot):
    page, target = jnp.int32(0), jnp.int32(-1)
    for m in range(NEWP):
        hit = new_owner[0, m] == place[0]
        page = jnp.where(hit, m, page)
        target = jnp.where(hit, new_slot[0, m], target)
    return page, target


def write_page(place, page, target, fresh, slots):
    x, y, way = (place[0] // 4) % 4, place[0] % 4, 1 - 2 * (place[1] & 1)
    row = lax.broadcasted_iota(jnp.int32, (CHUNKS, 128), 0)
    col = lax.broadcasted_iota(jnp.int32, (CHUNKS, 128), 1)
    holder = page * 8 + (row >> 2)
    part, block = gray((x - (holder >> 2)) & 3), gray(((y - holder) * way) & 3)
    source = block * 32 + part * 8 + (holder >> 4) * 4 + (row & 3)
    pick = (col == source).astype(jnp.float32).astype(jnp.bfloat16)
    rows = jnp.dot(pick, fresh, preferred_element_type=jnp.float32)
    rows = jnp.concatenate([rows[:, :VLAT], pltpu.roll(rows[:, VLAT:], LAT, 1)], axis=1)
    for low, high in ((0, 8), (8, SLOTS)):

        @pl.when((target >= low) & (target < high))
        def _():
            mine = lax.broadcasted_iota(jnp.int32, (high - low, PAIR), 0) + low == target
            for c in range(CHUNKS):
                columns = slice(c * PAIR, (c + 1) * PAIR)
                old = slots[low:high, columns].astype(jnp.float32)
                slots[low:high, columns] = jnp.where(mine, rows[c : c + 1], old).astype(jnp.bfloat16)


def attend_kernel(blocks, first, last, *refs):
    n = len(blocks)
    refs = list(refs)
    take = lambda count: [refs.pop(0) for _ in range(count)]
    place, length = take(2)
    new_owner, new_slot = take(2) if last else (None, None)
    even_q, odd_q = take(2)
    heads, tails = take(n), take(n)
    others, weights_in, pool = (take(4 - n), take(2), take(1)[0]) if last else ([], [], None)
    before = [] if first else take(2)
    after = take(2)
    keys = take(1)[0]

    if last:
        fresh, suffix, w, slots, moved = refs
        fill = pltpu.make_async_copy(pool, slots, moved.at[0])
        flush = pltpu.make_async_copy(slots, after[1], moved.at[1])
        fill.start()
    for b in range(n):
        for t in range(4):
            row = b * 128 + t * 32
            keys[row : row + 32] = heads[b][t * HEAD_ROWS : t * HEAD_ROWS + 32]
        keys[(n + b) * 128 : (n + b + 1) * 128] = tails[b][...]
    x, y, way = (place[0] // 4) % 4, place[0] % 4, 1 - 2 * (place[1] & 1)
    bias = [prefix_bias(blocks, parity, x, y, way, length[0]) for parity in range(2)]
    if last:
        for b, head in enumerate([*others, *heads]):
            for t in range(4):
                row = b * 32 + t * 8
                fresh[row : row + 8] = head[t * HEAD_ROWS + 32 : (t + 1) * HEAD_ROWS]
        suffix[:128] = fresh[:, : VLAT + 128]
        suffix[128:, :VLAT] = fresh[:, VLAT + 128 :]
        ropes = fresh[:, VLAT : VLAT + 128].astype(jnp.float32)
        suffix[128:, VLAT:] = pltpu.roll(ropes, 64, 1).astype(jnp.bfloat16)
        token = lax.broadcasted_iota(jnp.int32, (SUF, SUF), 0)
        hidden = suffix_order(x, y, way) > token
        for k in range(4):
            for other in range(2):
                part = ((place[1] // 2 - HOPS[k]) & 3) * 2 + ((place[1] & 1) ^ other)
                rows = pl.ds(pl.multiple_of(part * (VLAT // 8), VLAT // 8), VLAT // 8)
                w[:, rows, :] = weights_in[other][k]

    even = slice(0, VLAT), slice(0, VLAT + 128)
    odd = slice(VLAT + 128, PAIR), slice(VLAT, PAIR)
    groups = [(even_q, keys, even), (odd_q, keys, odd)]
    if last:
        groups.append((even_q, suffix, even))

    def scored(h):
        pieces = []
        for g, (queries, rows, (_, columns)) in enumerate(groups):
            s = lax.dot_general(
                queries[h], rows[:, columns], (((1,), (1,)), ((), ())), preferred_element_type=jnp.float32
            )
            pieces.append(jnp.where(hidden, masked_score, s) if g == 2 else s + bias[g])
        return pieces

    def mixed(h, pieces):
        top = pieces[0]
        for piece in pieces[1:]:
            top = jnp.maximum(top, piece)
        top = jnp.max(top, axis=1, keepdims=True)
        if not first:
            top_old, total_old = before[1][h, :, :1], before[1][h, :, 1:2]
            top = jnp.maximum(top, top_old)
        weights = [jnp.exp2((piece - top) * exponent_scale) for piece in pieces]
        total = jnp.sum(sum(weights[1:], weights[0]), axis=1, keepdims=True)
        parts = [
            jnp.dot(weight.astype(jnp.bfloat16), rows[:, columns], preferred_element_type=jnp.float32)
            for weight, (_, rows, (columns, _)) in zip(weights, groups)
        ]
        mixture = sum(parts[1:], parts[0])
        if not first:
            rescale = jnp.exp2((top_old - top) * exponent_scale)
            total = total + total_old * rescale
            mixture = mixture + before[0][h] * rescale
        if last:
            mixture = (mixture * (1.0 / total)).astype(jnp.bfloat16)
            out = jnp.dot(mixture, w[h], preferred_element_type=jnp.float32)
            after[0][:, h * VHEAD : (h + 1) * VHEAD] = out.astype(jnp.bfloat16)
        else:
            after[0][h] = mixture
            lane = lax.broadcasted_iota(jnp.int32, (SUF, 128), 1)
            after[1][h] = jnp.where(lane == 0, top, total)

    pieces = scored(0)
    for h in range(4):
        following = scored(h + 1) if h < 3 else None
        mixed(h, pieces)
        pieces = following
        if last and h == 1:
            page, target = new_page(place, new_owner, new_slot)
            fill.wait()

            @pl.when(target >= 0)
            def _():
                write_page(place, page, target, fresh[...], slots)

            flush.start()
    if last:
        flush.wait()


def attended(blocks, place, length, spread, heads, tails, state, ending=()):
    n, first, last = len(blocks), not state, bool(ending)
    whole = lambda *shape: pl.BlockSpec(shape, lambda h, *_: (0,) * len(shape))
    in_hbm = pl.BlockSpec(memory_space=pltpu.HBM)
    state_specs = [whole(4, SUF, VLAT), whole(4, SUF, 128)]
    own_heads, own_tails = [heads[b] for b in blocks], [tails[b] for b in blocks]
    others, w, tables, pool = [], [], (), []
    scratch = [pltpu.VMEM((256 * n, PAIR), jnp.bfloat16)]
    if last:
        w, new_owner, new_slot, pool = ending
        tables, pool = (new_owner, new_slot), [pool]
        others = [heads[b] for b in range(4) if b not in blocks]
        out_shape = [
            jax.ShapeDtypeStruct((SUF, 4 * VHEAD), jnp.bfloat16),
            jax.ShapeDtypeStruct((SLOTS, PAGE * LAT), jnp.bfloat16),
        ]
        out_specs = [whole(SUF, 4 * VHEAD), in_hbm]
        scratch += [
            pltpu.VMEM((128, PAIR), jnp.bfloat16),
            pltpu.VMEM((SUF, VLAT + 128), jnp.bfloat16),
            pltpu.VMEM((4, VLAT, VHEAD), jnp.bfloat16),
            pltpu.VMEM((SLOTS, PAGE * LAT), jnp.bfloat16),
            pltpu.SemaphoreType.DMA((2,)),
        ]
    else:
        out_shape = [
            jax.ShapeDtypeStruct((4, SUF, VLAT), jnp.float32),
            jax.ShapeDtypeStruct((4, SUF, 128), jnp.float32),
        ]
        out_specs = state_specs

    def kernel(*refs):
        attend_kernel(blocks, first, last, *refs)

    keys = 256 * n + (128 if last else 0)
    return pl.pallas_call(
        kernel,
        out_shape=out_shape,
        grid_spec=pltpu.PrefetchScalarGridSpec(
            num_scalar_prefetch=2 + len(tables),
            grid=(1,),
            in_specs=[
                *[whole(4, SUF, VLAT + 128)] * 2,
                *[whole(*a.shape) for a in (*own_heads, *own_tails, *others)],
                *[whole(4, 4, VLAT // 8, VHEAD)] * len(w),
                *[in_hbm] * len(pool),
                *([] if first else state_specs),
            ],
            out_specs=out_specs,
            scratch_shapes=scratch,
        ),
        compiler_params=pltpu.CompilerParams(vmem_limit_bytes=40 * MIB),
        cost_estimate=pl.CostEstimate(
            flops=8 * SUF * keys * (2 * VLAT + 128) * 2,
            transcendentals=8 * SUF * keys,
            bytes_accessed=16 * MIB,
        ),
        name="attend_" + "".join(str(b) for b in blocks),
    )(place, length, *tables, *spread, *own_heads, *own_tails, *others, *w, *pool, *state)


def local(queries, new_latent, pool, page_owner, page_slot, new_owner, new_slot, prefix_len, w_uv):
    place = jnp.stack([lax.axis_index(POOL), lax.axis_index(SERVE)]).astype(jnp.int32)
    w_row = jnp.stack([w_uv] + [shifted(w_uv, "serve_0", k) for k in HOPS[1:]])
    page_owner, page_slot, new_owner, new_slot, new_latent, in_place = (
        pltpu.with_memory_space_constraint(a, pltpu.HBM)
        for a in (page_owner, page_slot, new_owner, new_slot, new_latent, pool[0])
    )
    pieces, source, own = selected_pieces(place, page_owner, page_slot, in_place, new_latent)
    received = lax.all_to_all(pieces, PLANE, 0, 0, tiled=True).reshape(128, PAIR)
    mine = merged_rows(received, source, own)
    mine, queries = lax.optimization_barrier((mine, queries))
    spread = spread_queries(queries[0])
    both = mine + lax.ppermute(mine, "pool_0", [(0, 1), (1, 0)])
    both, w_row, spread = lax.optimization_barrier((both, w_row, spread))
    w = [w_row, lax.ppermute(w_row, "serve_1", [(0, 1), (1, 0)])]
    head, tail = both[:HEAD_ROWS], both[HEAD_ROWS:]
    head_parts = [shifted(head, "pool_1", k) for k in HOPS[1:]]
    tail_parts = [shifted(tail, "pool_2", k) for k in HOPS[1:]]
    head_parts, tail_parts[:2] = lax.optimization_barrier((head_parts, tail_parts[:2]))
    head_row = jnp.concatenate([head, *head_parts])
    tail_row = jnp.concatenate([tail, *tail_parts])
    tail_row, *w = lax.optimization_barrier((tail_row, *w))
    heads, tails = [head_row], [tail_row]
    state = attended((0,), place, prefix_len, spread, heads, tails, ())
    for rows, axis in ((heads, "pool_2"), (tails, "pool_1")):
        rows += [mirrored(rows[0], axis, 1), mirrored(rows[0], axis, 3)]
        rows.append(mirrored(rows[1], axis, 1))
    state = attended((1, 2), place, prefix_len, spread, heads, tails, state)
    ending = (w, new_owner, new_slot, in_place)
    out, updated = attended((3,), place, prefix_len, spread, heads, tails, state, ending)
    return (out[None], updated[None])


def solution(mesh):
    shape = (2, SIDE, SIDE, SIDE, 2)
    split = Mesh(mesh.devices.reshape(shape), (*POOL, *SERVE))
    placed = (
        P(SERVE, None, POOL),
        P(SERVE, POOL),
        P(SERVE, POOL, None),
        P(SERVE, None),
        P(SERVE, None),
        P(SERVE, None),
        P(SERVE, None),
        P(SERVE),
        P(POOL, SERVE, None),
    )
    return jax.shard_map(
        local,
        mesh=split,
        in_specs=placed,
        out_specs=(P(SERVE, None, POOL), P(SERVE, POOL, None)),
        check_vma=False,
    )
```

```python
import jax
import jax.numpy as jnp
from jax import lax
from jax.experimental import pallas as pl
from jax.experimental.pallas import tpu as pltpu
from jax.sharding import Mesh
from jax.sharding import PartitionSpec as P

VLAT = 512
VHEAD = 128
PAGE = 64
SUF = 256
HOT = 3
LAT = 576
PPAGES = 32
NEWP = 4
SLOTS = 12
PAIR = 2 * LAT
CHUNKS = PAGE * LAT // PAIR
POOL = ("pool_0", "pool_1", "pool_2")
PLANE = ("pool_1", "pool_2")
SERVE = ("serve_0", "serve_1")
SIDE = 4
HOPS = (0, 1, 3, 2)
HEAD_ROWS = 40
TAIL_ROWS = 32
KEYS = 16 * (HEAD_ROWS + TAIL_ROWS)

softmax_scale = 192.0 ** (-0.5)
exponent_scale = softmax_scale * 1.4426950408889634
masked_score = -1e30
MIB = 1 << 20


def select_kernel(place, owner_hbm, slot_hbm, pool_hbm, suffix_hbm, *refs):
    out_ref, source_ref, own_ref, rows, fresh, owner, slot, count, arrived = refs
    copies = [
        pltpu.make_async_copy(owner_hbm, owner, arrived.at[4]),
        pltpu.make_async_copy(slot_hbm, slot, arrived.at[5]),
        pltpu.make_async_copy(suffix_hbm, fresh, arrived.at[6]),
    ]
    for i in range(4):
        columns = slice(i * 8 * PAIR, (i + 1) * 8 * PAIR)
        copies.append(
            pltpu.make_async_copy(pool_hbm.at[:, columns], rows.at[:, columns], arrived.at[i])
        )
    for copy in copies:
        copy.start()
    me, depth = place[0], place[0] // 16
    for j in range(PPAGES):
        count[j] = 0
    copies[0].wait()
    copies[1].wait()
    row = lax.broadcasted_iota(jnp.int32, (PPAGES, 128), 0)
    source = jnp.full((PPAGES, 128), -8, jnp.int32)
    chosen = [jnp.int32(0)] * HOT
    for j in range(PPAGES):
        holder = owner[0, j]
        rank = count[holder]
        count[holder] = rank + 1
        chosen = [jnp.where((holder == me) & (rank == k), slot[0, j], chosen[k]) for k in range(HOT)]
        at = jnp.where(holder // 16 == depth, (holder % 16) * 8 + rank, -8)
        source = jnp.where(row == j, at, source)
    source_ref[...] = source
    copies[2].wait()
    suffix = fresh[...].astype(jnp.float32)
    row = lax.broadcasted_iota(jnp.int32, (8, PAIR), 0)
    own = jnp.zeros((8, PAIR), jnp.float32)
    for t in range(4):
        own = jnp.where(row == depth * 4 + t, suffix[:, t * PAIR : (t + 1) * PAIR], own)
    own_ref[...] = own
    row = lax.broadcasted_iota(jnp.int32, (8, SLOTS), 0) % 4
    col = lax.broadcasted_iota(jnp.int32, (8, SLOTS), 1)
    want = jnp.where(row == 0, chosen[0], jnp.where(row == 1, chosen[1], chosen[2]))
    pick = ((col == want) & (row < HOT)).astype(jnp.float32).astype(jnp.bfloat16)
    upper = lax.broadcasted_iota(jnp.int32, (8, PAIR), 0) < 4
    for d in range(16):
        if d % 4 == 0:
            copies[3 + d // 4].wait()
        both = rows[:, 2 * d * PAIR : (2 * d + 2) * PAIR]
        picked = jnp.dot(pick, both, preferred_element_type=jnp.float32)
        out_ref[d] = jnp.where(upper, picked[:, :PAIR], picked[:, PAIR:]).astype(jnp.bfloat16)


def selected_pieces(place, owner, slot, pool, suffix):
    in_hbm = pl.BlockSpec(memory_space=pltpu.HBM)
    whole = lambda *shape: pl.BlockSpec(shape, lambda i, *_: (0,) * len(shape))
    return pl.pallas_call(
        select_kernel,
        out_shape=[
            jax.ShapeDtypeStruct((16, 8, PAIR), jnp.bfloat16),
            jax.ShapeDtypeStruct((PPAGES, 128), jnp.int32),
            jax.ShapeDtypeStruct((8, PAIR), jnp.float32),
        ],
        grid_spec=pltpu.PrefetchScalarGridSpec(
            num_scalar_prefetch=1,
            grid=(1,),
            in_specs=[in_hbm] * 4,
            out_specs=[whole(16, 8, PAIR), whole(PPAGES, 128), whole(8, PAIR)],
            scratch_shapes=[
                pltpu.VMEM((SLOTS, PAGE * LAT), jnp.bfloat16),
                pltpu.VMEM((1, 4 * PAIR), jnp.bfloat16),
                pltpu.SMEM((1, PPAGES), jnp.int32),
                pltpu.SMEM((1, PPAGES), jnp.int32),
                pltpu.SMEM((PPAGES,), jnp.int32),
                pltpu.SemaphoreType.DMA((7,)),
            ],
        ),
        compiler_params=pltpu.CompilerParams(vmem_limit_bytes=32 * MIB),
        name="select_pages",
    )(place, owner, slot, pool, suffix)


def merge_kernel(received_ref, source_ref, own_ref, out_ref):
    col = lax.broadcasted_iota(jnp.int32, (PPAGES, 128), 1)
    received = received_ref[...]
    halves = []
    for p in range(2):
        pick = (col == source_ref[...] + 4 * p).astype(jnp.float32).astype(jnp.bfloat16)
        halves.append(jnp.dot(pick, received, preferred_element_type=jnp.float32))
    rows = jnp.concatenate([halves[0], own_ref[...], halves[1]], axis=0)
    turned = pltpu.roll(rows[:, VLAT:], LAT, 1)
    out_ref[:, :VLAT] = rows[:, :VLAT].astype(jnp.bfloat16)
    out_ref[:, VLAT : VLAT + 128] = turned[:, VLAT:].astype(jnp.bfloat16)
    out_ref[:, VLAT + 128 :] = turned[:, :VLAT].astype(jnp.bfloat16)


def merged_rows(received, source, own):
    whole = lambda *shape: pl.BlockSpec(shape, lambda i: (0,) * len(shape))
    rows = HEAD_ROWS + TAIL_ROWS
    return pl.pallas_call(
        merge_kernel,
        out_shape=jax.ShapeDtypeStruct((rows, PAIR), jnp.bfloat16),
        grid=(1,),
        in_specs=[whole(128, PAIR), whole(PPAGES, 128), whole(8, PAIR)],
        out_specs=whole(rows, PAIR),
        compiler_params=pltpu.CompilerParams(vmem_limit_bytes=32 * MIB),
        name="merge_pages",
    )(received, source, own)


def shifted(x, axis, hop):
    return lax.ppermute(x, axis, [(i, (i + hop) % SIDE) for i in range(SIDE)])


def mirrored(x, axis, hop):
    places = [(i, core) for i in range(SIDE) for core in range(2)]
    pairs = [(2 * i + c, 2 * ((i + hop * (1 - 2 * c)) % SIDE) + c) for i, c in places]
    return lax.ppermute(x, (axis, "serve_1"), pairs)


def gray(s):
    return s ^ (s >> 1)


def spread_kernel(q_ref, even_ref, odd_ref):
    lane = lax.broadcasted_iota(jnp.int32, (SUF, 128), 1)
    for h in range(4):
        if h % 2 == 0:
            whole = q_ref[:, h * LAT : h * LAT + LAT + 64].astype(jnp.float32)
        else:
            whole = q_ref[:, h * LAT - 64 : h * LAT + LAT].astype(jnp.float32)
            whole = pltpu.roll(whole, LAT, 1)
        latent = whole[:, :VLAT].astype(jnp.bfloat16)
        rest = whole[:, VLAT:]
        even_ref[h, :, :VLAT] = latent
        odd_ref[h, :, 128:] = latent
        odd_ref[h, :, :128] = jnp.where(lane < 64, rest, 0.0).astype(jnp.bfloat16)
        even_ref[h, :, VLAT:] = jnp.where(lane < 64, 0.0, pltpu.roll(rest, 64, 1)).astype(jnp.bfloat16)


def spread_queries(queries):
    shape = (4, SUF, VLAT + 128)
    return pl.pallas_call(
        spread_kernel,
        out_shape=[jax.ShapeDtypeStruct(shape, jnp.bfloat16)] * 2,
        grid=(1,),
        in_specs=[pl.BlockSpec((SUF, 4 * LAT), lambda i: (0, 0))],
        out_specs=[pl.BlockSpec(shape, lambda i: (0, 0, 0))] * 2,
        compiler_params=pltpu.CompilerParams(vmem_limit_bytes=32 * MIB),
        cost_estimate=pl.CostEstimate(flops=0, transcendentals=0, bytes_accessed=4 * MIB),
        name="spread_queries",
    )(queries)


def prefix_bias(blocks, parity, x, y, way, length):
    lane = lax.broadcasted_iota(jnp.int32, (1, 256 * len(blocks)), 1)
    part, page = (lane >> 5) & 3, lane & 31
    index = (lane >> 7) & (len(blocks) - 1)
    hop = jnp.full(lane.shape, HOPS[blocks[0]], jnp.int32)
    for n in range(1, len(blocks)):
        hop = jnp.where(index == n, HOPS[blocks[n]], hop)
    head = lane < 128 * len(blocks)
    turn = gray(part)
    hop = hop * way
    far = (x - jnp.where(head, turn, hop)) & 3
    near = (y - jnp.where(head, hop, turn)) & 3
    token = page * PAGE + (far * 4 + near) * 4 + jnp.where(head, 0, 2) + parity
    return jnp.where(token < length, 0.0, masked_score)


def suffix_order(x, y, way):
    lane = lax.broadcasted_iota(jnp.int32, (1, SUF), 1)
    block, part = (lane >> 5) & 3, (lane >> 3) & 3
    far, near = (x - gray(part)) & 3, (y - gray(block) * way) & 3
    holder = ((lane >> 2) & 1) * 16 + far * 4 + near
    return holder * 8 + (lane & 3) * 2 + (lane >> 7)


def new_page(place, new_owner, new_slot):
    page, target = jnp.int32(0), jnp.int32(-1)
    for m in range(NEWP):
        hit = new_owner[0, m] == place[0]
        page = jnp.where(hit, m, page)
        target = jnp.where(hit, new_slot[0, m], target)
    return page, target


def write_page(place, page, target, fresh, slots):
    x, y, way = (place[0] // 4) % 4, place[0] % 4, 1 - 2 * (place[1] & 1)
    row = lax.broadcasted_iota(jnp.int32, (CHUNKS, 128), 0)
    col = lax.broadcasted_iota(jnp.int32, (CHUNKS, 128), 1)
    holder = page * 8 + (row >> 2)
    part, block = gray((x - (holder >> 2)) & 3), gray(((y - holder) * way) & 3)
    source = block * 32 + part * 8 + (holder >> 4) * 4 + (row & 3)
    pick = (col == source).astype(jnp.float32).astype(jnp.bfloat16)
    rows = jnp.dot(pick, fresh, preferred_element_type=jnp.float32)
    rows = jnp.concatenate([rows[:, :VLAT], pltpu.roll(rows[:, VLAT:], LAT, 1)], axis=1)
    for low, high in ((0, 8), (8, SLOTS)):

        @pl.when((target >= low) & (target < high))
        def _():
            mine = lax.broadcasted_iota(jnp.int32, (high - low, PAIR), 0) + low == target
            for c in range(CHUNKS):
                columns = slice(c * PAIR, (c + 1) * PAIR)
                old = slots[low:high, columns].astype(jnp.float32)
                slots[low:high, columns] = jnp.where(mine, rows[c : c + 1], old).astype(jnp.bfloat16)


def attend_kernel(blocks, first, last, *refs):
    n = len(blocks)
    refs = list(refs)
    take = lambda count: [refs.pop(0) for _ in range(count)]
    place, length = take(2)
    new_owner, new_slot = take(2) if last else (None, None)
    even_q, odd_q = take(2)
    heads, tails = take(n), take(n)
    others, weights_in, pool = (take(4 - n), take(2), take(1)[0]) if last else ([], [], None)
    before = [] if first else take(2)
    after = take(2)
    keys = take(1)[0]

    if last:
        fresh, suffix, w, slots, moved = refs
        fill = pltpu.make_async_copy(pool, slots, moved.at[0])
        flush = pltpu.make_async_copy(slots, after[1], moved.at[1])
        fill.start()
    for b in range(n):
        for t in range(4):
            row = b * 128 + t * 32
            keys[row : row + 32] = heads[b][t * HEAD_ROWS : t * HEAD_ROWS + 32]
        keys[(n + b) * 128 : (n + b + 1) * 128] = tails[b][...]
    x, y, way = (place[0] // 4) % 4, place[0] % 4, 1 - 2 * (place[1] & 1)
    bias = [prefix_bias(blocks, parity, x, y, way, length[0]) for parity in range(2)]
    if last:
        for b, head in enumerate([*others, *heads]):
            for t in range(4):
                row = b * 32 + t * 8
                fresh[row : row + 8] = head[t * HEAD_ROWS + 32 : (t + 1) * HEAD_ROWS]
        suffix[:128] = fresh[:, : VLAT + 128]
        suffix[128:, :VLAT] = fresh[:, VLAT + 128 :]
        ropes = fresh[:, VLAT : VLAT + 128].astype(jnp.float32)
        suffix[128:, VLAT:] = pltpu.roll(ropes, 64, 1).astype(jnp.bfloat16)
        token = lax.broadcasted_iota(jnp.int32, (SUF, SUF), 0)
        hidden = suffix_order(x, y, way) > token
        for k in range(4):
            for other in range(2):
                part = ((place[1] // 2 - HOPS[k]) & 3) * 2 + ((place[1] & 1) ^ other)
                rows = pl.ds(pl.multiple_of(part * (VLAT // 8), VLAT // 8), VLAT // 8)
                w[:, rows, :] = weights_in[other][k]

    even = slice(0, VLAT), slice(0, VLAT + 128)
    odd = slice(VLAT + 128, PAIR), slice(VLAT, PAIR)
    groups = [(even_q, keys, even), (odd_q, keys, odd)]
    if last:
        groups.append((even_q, suffix, even))

    def scored(h):
        pieces = []
        for g, (queries, rows, (_, columns)) in enumerate(groups):
            s = lax.dot_general(
                queries[h], rows[:, columns], (((1,), (1,)), ((), ())), preferred_element_type=jnp.float32
            )
            pieces.append(jnp.where(hidden, masked_score, s) if g == 2 else s + bias[g])
        return pieces

    def mixed(h, pieces):
        top = pieces[0]
        for piece in pieces[1:]:
            top = jnp.maximum(top, piece)
        top = jnp.max(top, axis=1, keepdims=True)
        if not first:
            top_old, total_old = before[1][h, :, :1], before[1][h, :, 1:2]
            top = jnp.maximum(top, top_old)
        weights = [jnp.exp2((piece - top) * exponent_scale) for piece in pieces]
        total = jnp.sum(sum(weights[1:], weights[0]), axis=1, keepdims=True)
        parts = [
            jnp.dot(weight.astype(jnp.bfloat16), rows[:, columns], preferred_element_type=jnp.float32)
            for weight, (_, rows, (columns, _)) in zip(weights, groups)
        ]
        mixture = sum(parts[1:], parts[0])
        if not first:
            rescale = jnp.exp2((top_old - top) * exponent_scale)
            total = total + total_old * rescale
            mixture = mixture + before[0][h] * rescale
        if last:
            mixture = (mixture * (1.0 / total)).astype(jnp.bfloat16)
            out = jnp.dot(mixture, w[h], preferred_element_type=jnp.float32)
            after[0][:, h * VHEAD : (h + 1) * VHEAD] = out.astype(jnp.bfloat16)
        else:
            after[0][h] = mixture
            lane = lax.broadcasted_iota(jnp.int32, (SUF, 128), 1)
            after[1][h] = jnp.where(lane == 0, top, total)

    pieces = scored(0)
    for h in range(4):
        following = scored(h + 1) if h < 3 else None
        mixed(h, pieces)
        pieces = following
        if last and h == 1:
            page, target = new_page(place, new_owner, new_slot)
            fill.wait()

            @pl.when(target >= 0)
            def _():
                write_page(place, page, target, fresh[...], slots)

            flush.start()
    if last:
        flush.wait()


def attended(blocks, place, length, spread, heads, tails, state, ending=()):
    n, first, last = len(blocks), not state, bool(ending)
    whole = lambda *shape: pl.BlockSpec(shape, lambda h, *_: (0,) * len(shape))
    in_hbm = pl.BlockSpec(memory_space=pltpu.HBM)
    state_specs = [whole(4, SUF, VLAT), whole(4, SUF, 128)]
    own_heads, own_tails = [heads[b] for b in blocks], [tails[b] for b in blocks]
    others, w, tables, pool = [], [], (), []
    scratch = [pltpu.VMEM((256 * n, PAIR), jnp.bfloat16)]
    if last:
        w, new_owner, new_slot, pool = ending
        tables, pool = (new_owner, new_slot), [pool]
        others = [heads[b] for b in range(4) if b not in blocks]
        out_shape = [
            jax.ShapeDtypeStruct((SUF, 4 * VHEAD), jnp.bfloat16),
            jax.ShapeDtypeStruct((SLOTS, PAGE * LAT), jnp.bfloat16),
        ]
        out_specs = [whole(SUF, 4 * VHEAD), in_hbm]
        scratch += [
            pltpu.VMEM((128, PAIR), jnp.bfloat16),
            pltpu.VMEM((SUF, VLAT + 128), jnp.bfloat16),
            pltpu.VMEM((4, VLAT, VHEAD), jnp.bfloat16),
            pltpu.VMEM((SLOTS, PAGE * LAT), jnp.bfloat16),
            pltpu.SemaphoreType.DMA((2,)),
        ]
    else:
        out_shape = [
            jax.ShapeDtypeStruct((4, SUF, VLAT), jnp.float32),
            jax.ShapeDtypeStruct((4, SUF, 128), jnp.float32),
        ]
        out_specs = state_specs

    def kernel(*refs):
        attend_kernel(blocks, first, last, *refs)

    keys = 256 * n + (128 if last else 0)
    return pl.pallas_call(
        kernel,
        out_shape=out_shape,
        grid_spec=pltpu.PrefetchScalarGridSpec(
            num_scalar_prefetch=2 + len(tables),
            grid=(1,),
            in_specs=[
                *[whole(4, SUF, VLAT + 128)] * 2,
                *[whole(*a.shape) for a in (*own_heads, *own_tails, *others)],
                *[whole(4, 4, VLAT // 8, VHEAD)] * len(w),
                *[in_hbm] * len(pool),
                *([] if first else state_specs),
            ],
            out_specs=out_specs,
            scratch_shapes=scratch,
        ),
        compiler_params=pltpu.CompilerParams(vmem_limit_bytes=40 * MIB),
        cost_estimate=pl.CostEstimate(
            flops=8 * SUF * keys * (2 * VLAT + 128) * 2,
            transcendentals=8 * SUF * keys,
            bytes_accessed=16 * MIB,
        ),
        name="attend_" + "".join(str(b) for b in blocks),
    )(place, length, *tables, *spread, *own_heads, *own_tails, *others, *w, *pool, *state)


def local(queries, new_latent, pool, page_owner, page_slot, new_owner, new_slot, prefix_len, w_uv):
    place = jnp.stack([lax.axis_index(POOL), lax.axis_index(SERVE)]).astype(jnp.int32)
    w_row = jnp.stack([w_uv] + [shifted(w_uv, "serve_0", k) for k in HOPS[1:]])
    page_owner, page_slot, new_owner, new_slot, new_latent, in_place = (
        pltpu.with_memory_space_constraint(a, pltpu.HBM)
        for a in (page_owner, page_slot, new_owner, new_slot, new_latent, pool[0])
    )
    pieces, source, own = selected_pieces(place, page_owner, page_slot, in_place, new_latent)
    received = lax.all_to_all(pieces, PLANE, 0, 0, tiled=True).reshape(128, PAIR)
    mine = merged_rows(received, source, own)
    mine, queries = lax.optimization_barrier((mine, queries))
    spread = spread_queries(queries[0])
    both = mine + lax.ppermute(mine, "pool_0", [(0, 1), (1, 0)])
    both, w_row, spread = lax.optimization_barrier((both, w_row, spread))
    w = [w_row, lax.ppermute(w_row, "serve_1", [(0, 1), (1, 0)])]
    head, tail = both[:HEAD_ROWS], both[HEAD_ROWS:]
    head_parts = [shifted(head, "pool_1", k) for k in HOPS[1:]]
    tail_parts = [shifted(tail, "pool_2", k) for k in HOPS[1:]]
    head_parts, tail_parts[:2] = lax.optimization_barrier((head_parts, tail_parts[:2]))
    head_row = jnp.concatenate([head, *head_parts])
    tail_row = jnp.concatenate([tail, *tail_parts])
    tail_row, *w = lax.optimization_barrier((tail_row, *w))
    heads, tails = [head_row], [tail_row]
    state = attended((0,), place, prefix_len, spread, heads, tails, ())
    for rows, axis in ((heads, "pool_2"), (tails, "pool_1")):
        rows += [mirrored(rows[0], axis, 1), mirrored(rows[0], axis, 3)]
    heads.append(mirrored(heads[1], "pool_2", 1))
    state, tails[1:] = lax.optimization_barrier((state, tails[1:]))
    half = tail_row.shape[0] // 2
    far = mirrored(tails[1][:half], "pool_1", 1), mirrored(tails[2][half:], "pool_1", 3)
    tails.append(jnp.concatenate(far))
    state = attended((1, 2), place, prefix_len, spread, heads, tails, state)
    ending = (w, new_owner, new_slot, in_place)
    out, updated = attended((3,), place, prefix_len, spread, heads, tails, state, ending)
    return (out[None], updated[None])


def solution(mesh):
    shape = (2, SIDE, SIDE, SIDE, 2)
    split = Mesh(mesh.devices.reshape(shape), (*POOL, *SERVE))
    placed = (
        P(SERVE, None, POOL),
        P(SERVE, POOL),
        P(SERVE, POOL, None),
        P(SERVE, None),
        P(SERVE, None),
        P(SERVE, None),
        P(SERVE, None),
        P(SERVE),
        P(POOL, SERVE, None),
    )
    return jax.shard_map(
        local,
        mesh=split,
        in_specs=placed,
        out_specs=(P(SERVE, None, POOL), P(SERVE, POOL, None)),
        check_vma=False,
    )
```
